256 devices in a mesh: gx: 32 (over z, y), gy: 8 (over x, core).
Axes of the slice: x: 4, y: 4, z: 8, core: 2. Of those that a mesh axis runs over, the one named last changes fastest.
Arguments:
- efield: float32 [3, 512, 256, 128], P(None, 'gx', 'gy'), may hold values from -6 to 6
- hfield: float32 [3, 512, 256, 128], P(None, 'gx', 'gy'), may hold values from -6 to 6
- polar: float32 [3, 512, 256, 128], P(None, 'gx', 'gy'), may hold values from -6 to 6
- material_map: int32 [512, 256, 128], P('gx', 'gy'), may hold values from 0 to 2
- via_index: int32 [512, 256, 128], P('gx', 'gy'), may hold values from 0 to 7
- fill_fraction: float32 [512, 256, 128], P('gx', 'gy'), may hold values from 0 to 1
- permittivity: float32 [3], replicated, may hold values from 1 to 5
- conductivity: float32 [3], replicated, may hold values from 0 to 2
- debye_strength: float32 [3], replicated, may hold values from 0.5 to 3
- relax_time: float32 [3], replicated, may hold values from 0.5 to 5
- conformal: float32 [8, 3], replicated, may hold values from 0.3 to 1
Outputs:
- efield_out: float32 [3, 512, 256, 128], P(None, 'gx', 'gy')
- hfield_out: float32 [3, 512, 256, 128], P(None, 'gx', 'gy')
- polar_out: float32 [3, 512, 256, 128], P(None, 'gx', 'gy')
The draws below stay inside these ranges and needn't reach their ends.
Inputs may be any that keep to these rules, and one draw needn't show every extreme that they name: `via_index`: a row of the conformal table.
All inputs are finite; a program needn't handle non-finite values.
Results may differ from the reference program's by a relative error of at most 0.00002.
Values sent between devices are 32-bit elements; how exact they have to be, the bound alone decides.
No kernel may reach another device: no remote copies, remote signals or barrier semaphores. Data moves between devices by JAX's collectives and lax.ppermute only.
A program may use at most 64 MiB of HBM per device.

```python
import math
import jax
import jax.numpy as jnp
from jax import lax

NZ = 128
STEPS = 4
NMAT = 3
VIAS = 8
NX = 512
NY = 256


def touch_ends(values, stream_key, least, high):
    dims = values.shape
    spot = [jax.random.randint(jax.random.fold_in(stream_key, axis), (), 0, dims[axis]) for axis in range(len(dims))]
    values = values.at[tuple(spot)].set(least)
    longest = dims.index(max(dims))
    spot[longest] = (spot[longest] + 1) % dims[longest]
    return values.at[tuple(spot)].set(high)


def shard_levels(own_key, dims, shards, least, largest):
    def one(axis_at, blocks):
        heights = jax.random.uniform(jax.random.fold_in(jax.random.fold_in(own_key, 6), axis_at), (blocks,), jnp.float32, least / len(shards), largest / len(shards))
        return jnp.repeat(jnp.exp(heights), dims[axis_at] // blocks).reshape((-1,) + (1,) * (len(dims) - axis_at - 1))

    factor_of = one(*shards[0])
    for cut in shards[1:]:
        factor_of = factor_of * one(*cut)
    return factor_of


def bell_draw(key, extent, spread, bound, shards=(), kind=jnp.bfloat16):
    entries = jax.random.normal(key, extent, jnp.float32) * spread
    if len(shards) > 0:
        entries = shard_levels(key, extent, shards, -0.22, 0.18) * entries
    return jnp.clip(entries, min=-bound, max=bound).astype(kind)


def setup_inputs(seed: int = 0) -> dict:
    keys = jax.random.split(jax.random.key(seed), 12)
    return {
        "efield": bell_draw(keys[0], (3, NX, NY, NZ), 1.0, 6.0, ((1, 32), (2, 8)), jnp.float32),
        "hfield": bell_draw(keys[1], (3, NX, NY, NZ), 1.0, 6.0, ((1, 32), (2, 8)), jnp.float32),
        "polar": bell_draw(keys[2], (3, NX, NY, NZ), 1.0, 6.0, ((1, 32), (2, 8)), jnp.float32),
        "material_map": touch_ends(jax.random.randint(keys[3], (NX, NY, NZ), 0, 3), jax.random.fold_in(keys[3], 1), 0, 2).astype(jnp.int32),
        "via_index": touch_ends(jax.random.randint(keys[4], (NX, NY, NZ), 0, VIAS), jax.random.fold_in(keys[4], 1), 0, VIAS - 1).astype(jnp.int32),
        "fill_fraction": jnp.clip(1.0 * jax.random.uniform(keys[5], (NX, NY, NZ), jnp.float32) ** shard_levels(keys[5], (NX, NY, NZ), ((0, 32), (1, 8)), -0.2, 0.2), 0.0, 1.0),
        "permittivity": jnp.clip(jnp.exp(jax.random.uniform(keys[6], (NMAT,), jnp.float32, math.log(1.0), math.log(5.0))), 1.0, 5.0),
        "conductivity": jnp.clip(jax.random.uniform(keys[7], (NMAT,), jnp.float32, 0.0, 2.0), 0.0, 2.0),
        "debye_strength": jnp.clip(jax.random.uniform(keys[8], (NMAT,), jnp.float32, 0.5, 3.0), 0.5, 3.0),
        "relax_time": jnp.clip(jnp.exp(jax.random.uniform(keys[9], (NMAT,), jnp.float32, math.log(0.5), math.log(5.0))), 0.5, 5.0),
        "conformal": jnp.clip(jax.random.uniform(keys[10], (VIAS, 3), jnp.float32, 0.3, 1.0), 0.3, 1.0),
    }


time_step = 0.55


def select(ids, table, count):
    total = jnp.zeros(ids.shape, jnp.float32)
    for entry in range(count):
        total = total + jnp.where(ids == entry, table[entry], jnp.zeros((), table.dtype))
    return total


def coefficients(material_map, via_index, fill_fraction, permittivity, conductivity, debye_strength, relax_time, conformal):
    count = permittivity.shape[0]
    eps = select(material_map, permittivity, count) * (1.0 + fill_fraction)
    loss = select(material_map, conductivity, count) * time_step / (2.0 * eps)
    ca_coef = (1.0 - loss) / (1.0 + loss)
    cb_coef = time_step / (eps * (1.0 + loss))
    cbp_coef = cb_coef / time_step
    relax = select(material_map, relax_time, count)
    kp_coef = (2.0 * relax - time_step) / (2.0 * relax + time_step)
    bp_coef = 2.0 * time_step * select(material_map, debye_strength, count) / (2.0 * relax + time_step)
    vias = conformal.shape[0]
    weights = [cb_coef * select(via_index, conformal[:, comp], vias) for comp in range(3)]
    return jnp.stack([ca_coef, cbp_coef, kp_coef, bp_coef] + weights)


def forward(field, axis, plane):
    rest = lax.slice_in_dim(field, 1, field.shape[axis], axis=axis)
    return jnp.concatenate([rest, plane], axis=axis)


def backward(field, axis, plane):
    rest = lax.slice_in_dim(field, 0, field.shape[axis] - 1, axis=axis)
    return jnp.concatenate([plane, rest], axis=axis)


def curl_e(efield, y_next, x_next):
    ex_comp, ey_comp, ez_comp = efield[0], efield[1], efield[2]
    z_plane = jnp.zeros_like(ex_comp[:, :, :1])
    cx_part = (forward(ez_comp, 1, y_next[1]) - ez_comp) - (forward(ey_comp, 2, z_plane) - ey_comp)
    cy_part = (forward(ex_comp, 2, z_plane) - ex_comp) - (forward(ez_comp, 0, x_next[1]) - ez_comp)
    cz_part = (forward(ey_comp, 0, x_next[0]) - ey_comp) - (forward(ex_comp, 1, y_next[0]) - ex_comp)
    return jnp.stack([cx_part, cy_part, cz_part])


def curl_h(hfield, y_prev, x_prev):
    hx_comp, hy_comp, hz_comp = hfield[0], hfield[1], hfield[2]
    z_plane = jnp.zeros_like(hx_comp[:, :, :1])
    cx_part = (hz_comp - backward(hz_comp, 1, y_prev[1])) - (hy_comp - backward(hy_comp, 2, z_plane))
    cy_part = (hx_comp - backward(hx_comp, 2, z_plane)) - (hz_comp - backward(hz_comp, 0, x_prev[1]))
    cz_part = (hy_comp - backward(hy_comp, 0, x_prev[0])) - (hx_comp - backward(hx_comp, 1, y_prev[0]))
    return jnp.stack([cx_part, cy_part, cz_part])


def reference(efield, hfield, polar, material_map, via_index, fill_fraction, permittivity, conductivity, debye_strength, relax_time, conformal):
    coef = coefficients(material_map, via_index, fill_fraction, permittivity, conductivity, debye_strength, relax_time, conformal)
    elec, magn, pol = efield, hfield, polar
    y_zero = jnp.zeros_like(elec[0:2, :, :1])
    x_zero = jnp.zeros_like(elec[0:2, :1])
    for step in range(STEPS):
        magn = magn - time_step * curl_e(elec, y_zero, x_zero)
        pol_new = coef[2] * pol + coef[3] * elec
        elec = coef[0] * elec + coef[4:7] * curl_h(magn, y_zero, x_zero) - coef[1] * (pol_new - pol)
        pol = pol_new
    return elec, magn, pol
```

```python
import jax
import jax.numpy as jnp
from jax import lax
from jax.experimental import pallas as pl
from jax.experimental.pallas import tpu as pltpu
from jax.sharding import PartitionSpec as P

STEPS = 4
DT = 0.55
HALO = 4
F32 = jnp.float32

NXL, NYL, NZ = 16, 32, 128
NXE, NYE = NXL + 2 * HALO, NYL + 8

NMSG = 41


def swapped(value, axis, first):
    size = lax.axis_size(axis)
    pairs = []
    for low in range(first, size - 1, 2):
        pairs += [(low, low + 1), (low + 1, low)]
    return lax.ppermute(value, axis, pairs)


def plane_parts():
    parts = [("e", c, 4, 4 * c) for c in range(3)]
    parts += [("h", 1, 4, 12), ("h", 2, 4, 16), ("h", 0, 3, 20)]
    parts += [("p", c, 3, 23 + 3 * c) for c in range(3)]
    parts += [("c", c, 3, 32 + 3 * c) for c in range(3)]
    return parts


def pack_gx(e, h, p, mat, via, fill, out_a, out_b, ints, sems):
    parity = lax.axis_index("gx") % 2
    src = {"e": e, "h": h, "p": p}
    copies = []
    for which, out in enumerate((out_a, out_b)):
        upward = parity == which
        s4 = jnp.where(upward, NXL - 4, 0)
        s3 = jnp.where(upward, NXL - 3, 0)
        for name, c, n, at in plane_parts():
            s = s4 if n == 4 else s3
            if name == "c":
                ref = (mat, via, fill)[c].at[pl.ds(s, n)]
                dst = out.at[pl.ds(at, n)] if c == 2 else ints.at[which, c]
            else:
                ref = src[name].at[c, pl.ds(s, n)]
                dst = out.at[pl.ds(at, n)]
            copies.append(pltpu.make_async_copy(ref, dst, sems.at[len(copies)]))
    for copy in copies:
        copy.start()
    for copy in copies:
        copy.wait()
    for which, out in enumerate((out_a, out_b)):
        out[32:35] = ints[which, 0].astype(F32)
        out[35:38] = ints[which, 1].astype(F32)


def row_ids():
    return lax.broadcasted_iota(jnp.int32, (8, NZ), 0)


def pack_gy(e, h, p, mat, via, fill, out_c, out_d, rows, irows, sems):
    parity = lax.axis_index("gy") % 2
    copies = []
    for which in range(2):
        upward = parity == which
        r = pl.multiple_of(jnp.where(upward, NYL - 8, 0), 8)
        for k, ref in enumerate((e, h, p)):
            copies.append((ref.at[:, :, pl.ds(r, 8)], rows.at[which, pl.ds(3 * k, 3)]))
        copies.append((fill.at[:, pl.ds(r, 8)], rows.at[which, 9]))
        copies.append((mat.at[:, pl.ds(r, 8)], irows.at[which, 0]))
        copies.append((via.at[:, pl.ds(r, 8)], irows.at[which, 1]))
    copies = [pltpu.make_async_copy(a, b, sems.at[i]) for i, (a, b) in enumerate(copies)]
    for copy in copies:
        copy.start()
    for copy in copies:
        copy.wait()
    low = row_ids() < 4
    for which, out in enumerate((out_c, out_d)):
        upward = parity == which

        def body(x, _):
            tiles = [rows[which, k, x] for k in range(10)]
            tiles += [irows[which, k, x].astype(F32) for k in range(2)]
            for k in range(6):
                a, b = tiles[2 * k], tiles[2 * k + 1]
                up = jnp.where(low, pltpu.roll(a, 4, 0), b)
                down = jnp.where(low, a, pltpu.roll(b, 4, 0))
                out[k, x] = jnp.where(upward, up, down)
            return 0

        lax.fori_loop(0, NXL, body, 0, unroll=2)


def halo_tile(from_c, from_d, parity, k, x):
    low = row_ids() < 4
    c, d = from_c[k, x], from_d[k, x]
    above = jnp.where(parity == 0, c, d)
    below = jnp.where(parity == 0, d, c)
    return (
        jnp.where(low, above, pltpu.roll(below, 4, 0)),
        jnp.where(low, pltpu.roll(above, 4, 0), below),
    )


ORDER = [("e", 0), ("e", 1), ("e", 2), ("h", 0), ("h", 1), ("h", 2), ("p", 0), ("p", 1), ("p", 2), ("c", 2), ("c", 0), ("c", 1)]


def pack_corner(from_c, from_d, out_a, out_b):
    ypar = lax.axis_index("gy") % 2
    parity = lax.axis_index("gx") % 2
    place = {(n, c): (planes, at) for n, c, planes, at in plane_parts()}
    for which, out in enumerate((out_a, out_b)):
        upward = parity == which
        s4 = jnp.where(upward, NXL - 4, 0)
        s3 = jnp.where(upward, NXL - 3, 0)
        for k in range(6):
            pair = [place[ORDER[2 * k]], place[ORDER[2 * k + 1]]]
            for i in range(4):
                tiles = {}
                for j, (planes, at) in enumerate(pair):
                    if i >= planes:
                        continue
                    if planes not in tiles:
                        s = s4 if planes == 4 else s3
                        tiles[planes] = halo_tile(from_c, from_d, ypar, k, s + i)
                    out[at + i] = tiles[planes][j]


def steps_kernel(
    e, h, p, mat, via, fill, perm, cond, stre, rlx, conf,
    got_a, got_b, row_c, row_d, cor_a, cor_b,
    e_out, h_out, p_out,
    ex, hx, px, cells, fills, w, sems,
):
    gx, gy = lax.axis_index("gx"), lax.axis_index("gy")
    nx, ny = lax.axis_size("gx"), lax.axis_size("gy")
    own = pl.ds(HALO, NXL)
    rows = pl.ds(0, NYL)
    loads = []
    for src, dst in ((e, ex), (h, hx), (p, px)):
        loads.append((src, dst.at[:, own, rows]))
    loads += [(mat, cells.at[0, own, rows]), (via, cells.at[1, own, rows]), (fill, fills.at[own, rows])]
    loads = [pltpu.make_async_copy(a, b, sems.at[i]) for i, (a, b) in enumerate(loads)]
    for copy in loads:
        copy.start()

    ext = {"e": ex, "h": hx, "p": px}

    def put(name, c, at, n, rws, value):
        if name == "c":
            if c == 2:
                fills[pl.ds(at, n), rws] = value
            else:
                cells[c, pl.ds(at, n), rws] = value.astype(jnp.int32)
        else:
            ext[name][c, pl.ds(at, n), rws] = value

    for which, (slab, corner) in enumerate(((got_a, cor_a), (got_b, cor_b))):
        from_above = gx % 2 == which
        d4 = jnp.where(from_above, HALO + NXL, 0)
        d3 = jnp.where(from_above, HALO + NXL, 1)
        for name, c, n, at in plane_parts():
            d = d4 if n == 4 else d3
            put(name, c, d, n, slice(0, NYL), slab[at:at + n])
            put(name, c, d, n, slice(NYL, NYE), corner[at:at + n])

    def rows_body(x, _):
        for k in range(6):
            pair = halo_tile(row_c, row_d, gy % 2, k, x)
            for j in range(2):
                name, c = ORDER[2 * k + j]
                if name == "c":
                    if c == 2:
                        fills[x + HALO, NYL:] = pair[j]
                    else:
                        cells[c, x + HALO, NYL:] = pair[j].astype(jnp.int32)
                else:
                    ext[name][c, x + HALO, NYL:] = pair[j]
        return 0

    lax.fori_loop(0, NXL, rows_body, 0, unroll=2)

    for copy in loads:
        copy.wait()

    row = lax.broadcasted_iota(jnp.int32, (NYE, NZ), 0)
    off_above = (row >= NYL) & (row < NYL + 4) & (gy == ny - 1)
    off_below = (row >= NYL + 4) & (gy == 0)
    row_in = jnp.where(off_above | off_below, 0.0, 1.0).astype(F32)
    lane = lax.broadcasted_iota(jnp.int32, (NYE, NZ), 1)
    last, first = lane == NZ - 1, lane == 0

    def plane_in(x):
        out = ((x < HALO) & (gx == 0)) | ((x >= HALO + NXL) & (gx == nx - 1))
        return jnp.where(out, 0.0, 1.0).astype(F32)

    def full(value):
        return jnp.full((8, NZ), value, F32)

    mats = []
    for m in range(3):
        tau = full(rlx[m])
        inv = 1.0 / (2.0 * tau + DT)
        mats.append((full(perm[m]), full(cond[m]) * (DT / 2), (2.0 * tau - DT) * inv, 2.0 * DT * full(stre[m]) * inv, 2.0 * DT * inv))
    lane8 = lax.broadcasted_iota(jnp.int32, (8, NZ), 1)
    tables = []
    for c in range(3):
        table = jnp.zeros((8, NZ), F32)
        for v in range(8):
            table = jnp.where(lane8 == v, conf[v, c], table)
        tables.append(table)

    def coef_body(x, _):
        inside = plane_in(x)
        for t in range(NYE // 8):
            r = slice(8 * t, 8 * t + 8)
            m, v, f = cells[0, x, r], cells[1, x, r], fills[x, r]
            m0, m1 = m == 0, m == 1
            pe, s, kp, bp, omk = (jnp.where(m0, mats[0][i], jnp.where(m1, mats[1][i], mats[2][i])) for i in range(5))
            eps = pe * (1.0 + f)
            inv = 1.0 / (eps + s)
            w[0, x, r] = (eps - s) * inv - inv * bp
            w[1, x, r] = inv * omk
            w[2, x, r] = kp
            w[3, x, r] = bp
            scale = inv * (DT * inside)
            if t == NYE // 8 - 1:
                scale = scale * row_in[r]
            for c in range(3):
                w[4 + c, x, r] = scale * jnp.take_along_axis(tables[c], v, axis=1)
        return 0

    lax.fori_loop(1, NXE - 1, coef_body, 0)

    def yf(a):
        return pltpu.roll(a, NYE - 1, 0)

    def yb(a):
        return pltpu.roll(a, 1, 0)

    def zf(a):
        return jnp.where(last, 0.0, pltpu.roll(a, NZ - 1, 1))

    def zb(a):
        return jnp.where(first, 0.0, pltpu.roll(a, 1, 1))

    def h_plane(x):
        m = row_in * (DT * plane_in(x))
        e0, e1, e2 = ex[0, x], ex[1, x], ex[2, x]
        h0 = hx[0, x] - m * ((yf(e2) - e2) - (zf(e1) - e1))
        h1 = hx[1, x] - m * ((zf(e0) - e0) - (ex[2, x + 1] - e2))
        h2 = hx[2, x] - m * ((ex[1, x + 1] - e1) - (yf(e0) - e0))
        hx[0, x], hx[1, x], hx[2, x] = h0, h1, h2
        return h0, h1, h2

    def e_plane(x, now, before):
        h0, h1, h2 = now
        curl = (
            (h2 - yb(h2)) - (h1 - zb(h1)),
            (h0 - zb(h0)) - (h2 - before[1]),
            (h1 - before[0]) - (h0 - yb(h0)),
        )
        for c in range(3):
            a, b = ex[c, x], px[c, x]
            ex[c, x] = w[0, x] * a + w[1, x] * b + w[4 + c, x] * curl[c]
            px[c, x] = w[2, x] * b + w[3, x] * a

    for step in range(STEPS):
        lo = step
        hi = NXE - 1 - step
        _, h1, h2 = h_plane(lo)

        def body(x, before):
            now = h_plane(x)
            e_plane(x, now, before)
            return now[1], now[2]

        lax.fori_loop(lo + 1, hi, body, (h1, h2))

    stores = []
    for src, dst in ((ex, e_out), (hx, h_out), (px, p_out)):
        stores.append(pltpu.make_async_copy(src.at[:, own, rows], dst, sems.at[len(stores)]))
    for copy in stores:
        copy.start()
    for copy in stores:
        copy.wait()


def shards(efield, hfield, polar, material_map, via_index, fill_fraction, permittivity, conductivity, debye_strength, relax_time, conformal):
    anywhere = pl.BlockSpec(memory_space=pl.ANY)
    vmem = pl.BlockSpec(memory_space=pltpu.VMEM)
    smem = pl.BlockSpec(memory_space=pltpu.SMEM)
    cells = (efield, hfield, polar, material_map, via_index, fill_fraction)
    slab = jax.ShapeDtypeStruct((NMSG, NYL, NZ), F32)
    strip = jax.ShapeDtypeStruct((6, NXL, 8, NZ), F32)
    corner = jax.ShapeDtypeStruct((NMSG, 8, NZ), F32)
    field = jax.ShapeDtypeStruct((3, NXL, NYL, NZ), F32)
    slab_a, slab_b = pl.pallas_call(
        pack_gx, out_shape=(slab, slab), in_specs=[anywhere] * 6, out_specs=(vmem, vmem),
        scratch_shapes=[pltpu.VMEM((2, 2, 3, NYL, NZ), jnp.int32), pltpu.SemaphoreType.DMA((24,))],
        name="pack_gx",
    )(*cells)
    strip_c, strip_d = pl.pallas_call(
        pack_gy, out_shape=(strip, strip), in_specs=[anywhere] * 6, out_specs=(vmem, vmem),
        scratch_shapes=[pltpu.VMEM((2, 10, NXL, 8, NZ), F32), pltpu.VMEM((2, 2, NXL, 8, NZ), jnp.int32), pltpu.SemaphoreType.DMA((12,))],
        name="pack_gy",
    )(*cells)
    got_b = swapped(slab_b, "gx", 1)
    got_a = swapped(slab_a, "gx", 0)
    row_c = swapped(strip_c, "gy", 0)
    row_d = swapped(strip_d, "gy", 1)
    corner_a, corner_b = pl.pallas_call(
        pack_corner, out_shape=(corner, corner), in_specs=[vmem] * 2, out_specs=(vmem, vmem), name="pack_corner",
    )(row_c, row_d)
    cor_b = swapped(corner_b, "gx", 1)
    cor_a = swapped(corner_a, "gx", 0)
    ext = (NXE, NYE, NZ)
    return pl.pallas_call(
        steps_kernel, out_shape=(field,) * 3,
        in_specs=[anywhere] * 6 + [smem] * 5 + [vmem] * 6, out_specs=(anywhere,) * 3,
        scratch_shapes=[
            pltpu.VMEM((3,) + ext, F32), pltpu.VMEM((3,) + ext, F32), pltpu.VMEM((3,) + ext, F32),
            pltpu.VMEM((2,) + ext, jnp.int32), pltpu.VMEM(ext, F32), pltpu.VMEM((7,) + ext, F32),
            pltpu.SemaphoreType.DMA((6,)),
        ],
        compiler_params=pltpu.CompilerParams(vmem_limit_bytes=40 << 20),
        name="steps",
    )(*cells, permittivity, conductivity, debye_strength, relax_time, conformal, got_a, got_b, row_c, row_d, cor_a, cor_b)


def solution(mesh):
    whole, cell = P(None, "gx", "gy", None), P("gx", "gy", None)
    return jax.shard_map(
        shards, mesh=mesh, in_specs=(whole,) * 3 + (cell,) * 3 + (P(),) * 5, out_specs=(whole,) * 3, check_vma=False,
    )
```

```python
import jax
import jax.numpy as jnp
from jax import lax
from jax.experimental import pallas as pl
from jax.experimental.pallas import tpu as pltpu
from jax.sharding import PartitionSpec as P

DT = 0.55
F32 = jnp.float32

NX, NY, NZ = 16, 32, 128
LOW, HIGH = 3, 2
R0, RH, RE = 8, 8 + NY, 16 + NY
EXT = (NX + LOW + HIGH, RE + 8, NZ)
TILES = (RE - R0) // 8
MSG1, MSG2 = 18, 8
MSG2_ROWS = MSG2 * (RE - R0) + MSG1 * 8

ORDER = (("e", 0), ("e", 1), ("e", 2), ("h", 0), ("h", 1), ("h", 2), ("p", 0), ("p", 1), ("p", 2), ("f", 0), ("c", 0), ("c", 1))


def swapped(value, axis, first):
    pairs = []
    for low in range(first, lax.axis_size(axis) - 1, 2):
        pairs += [(low, low + 1), (low + 1, low)]
    return lax.ppermute(value, axis, pairs)


def tile_iota(dim):
    return lax.broadcasted_iota(jnp.int32, (8, NZ), dim)


def materials(perm, cond, stre, rlx):
    out = []
    for m in range(3):
        tau = jnp.full((8, NZ), rlx[m], F32)
        inv = 1.0 / (2.0 * tau + DT)
        out.append((
            jnp.full((8, NZ), perm[m], F32), jnp.full((8, NZ), cond[m] * (DT / 2), F32),
            (2.0 * tau - DT) * inv, jnp.full((8, NZ), stre[m], F32) * (2.0 * DT) * inv, 2.0 * DT * inv,
        ))
    return out


def pick(mats, m, i):
    return jnp.where(m == 0, mats[0][i], jnp.where(m == 1, mats[1][i], mats[2][i]))


def via_tables(conf):
    lane = tile_iota(1)
    tables = []
    for c in range(3):
        table = jnp.zeros((8, NZ), F32)
        for v in range(8):
            table = jnp.where(lane == v, conf[c, v], table)
        tables.append(table)
    return tables


class Block:
    def __init__(self, ex, hx, px, cx, fx, w=None):
        self.e, self.h, self.p, self.c, self.f, self.w = ex, hx, px, cx, fx, w

    def masks(self):
        gy = lax.axis_index("gy")
        row = tile_iota(0)
        out = ((row < 4) & (gy == lax.axis_size("gy") - 1)) | ((row >= 4) & (gy == 0))
        self.row_in = jnp.where(out, 0.0, 1.0).astype(F32)
        lane = tile_iota(1)
        self.last, self.first = lane == NZ - 1, lane == 0

    def plane_in(self, x):
        if not isinstance(x, int) or 0 <= x < NX:
            return None
        gx = lax.axis_index("gx")
        out = gx == 0 if x < 0 else gx == lax.axis_size("gx") - 1
        return jnp.where(out, 0.0, 1.0).astype(F32)

    def zf(self, a):
        return jnp.where(self.last, 0.0, pltpu.roll(a, NZ - 1, 1))

    def zb(self, a):
        return jnp.where(self.first, 0.0, pltpu.roll(a, 1, 1))

    def coef(self, x, mats, tables):
        i = x + LOW
        inside = self.plane_in(x)
        for t in range(TILES):
            r = slice(R0 + 8 * t, R0 + 8 * t + 8)
            m, v, f = self.c[0, i, r], self.c[1, i, r], self.f[0, i, r]
            pe, s, kp, bp, omk = (pick(mats, m, k) for k in range(5))
            eps = pe * (1.0 + f)
            inv = 1.0 / (eps + s)
            self.w[0, i, r] = (eps - s) * inv - inv * bp
            self.w[1, i, r] = inv * omk
            self.w[2, i, r] = kp
            self.w[3, i, r] = bp
            scale = inv * DT if inside is None else inv * (DT * inside)
            if t == TILES - 1:
                scale = scale * self.row_in
            for c in range(3):
                self.w[4 + c, i, r] = scale * jnp.take_along_axis(tables[c], v, axis=1)

    def guard_e(self, i):
        for c in (0, 2):
            self.e[c, i, RE:RE + 1] = self.e[c, i, R0:R0 + 1]

    def h_plane(self, x):
        i = x + LOW
        e, h = self.e, self.h
        inside = self.plane_in(x)
        for t in range(TILES):
            a = R0 + 8 * t
            r, up = slice(a, a + 8), slice(a + 1, a + 9)
            e0, e1, e2 = e[0, i, r], e[1, i, r], e[2, i, r]
            m = DT if inside is None else DT * inside
            if t == TILES - 1:
                m = self.row_in * m
            h0 = h[0, i, r] - m * ((e[2, i, up] - e2) - (self.zf(e1) - e1))
            h1 = h[1, i, r] - m * ((self.zf(e0) - e0) - (e[2, i + 1, r] - e2))
            h2 = h[2, i, r] - m * ((e[1, i + 1, r] - e1) - (e[0, i, up] - e0))
            h[0, i, r], h[1, i, r], h[2, i, r] = h0, h1, h2
        h[0, i, R0 - 1:R0] = h0[7:8]
        h[2, i, R0 - 1:R0] = h2[7:8]

    def e_plane(self, x):
        i = x + LOW
        e, h, p, w = self.e, self.h, self.p, self.w
        for t in range(TILES):
            a = R0 + 8 * t
            r, down = slice(a, a + 8), slice(a - 1, a + 7)
            h0, h1, h2 = h[0, i, r], h[1, i, r], h[2, i, r]
            curl = (
                (h2 - h[2, i, down]) - (h1 - self.zb(h1)),
                (h0 - self.zb(h0)) - (h2 - h[2, i - 1, r]),
                (h1 - h[1, i - 1, r]) - (h0 - h[0, i, down]),
            )
            w0, w1, w2, w3 = (w[k, i, r] for k in range(4))
            for c in range(3):
                ec, pc = e[c, i, r], p[c, i, r]
                new = w0 * ec + w1 * pc + w[4 + c, i, r] * curl[c]
                e[c, i, r] = new
                p[c, i, r] = w2 * pc + w3 * ec
                if t == 0 and c != 1:
                    e[c, i, RE:RE + 1] = new[0:1]

    def sweep(self, h_planes, e_planes):
        for x in range(min(h_planes[0], e_planes[0]), max(h_planes[1], e_planes[1]) + 1):
            if h_planes[0] <= x <= h_planes[1]:
                self.h_plane(x)
            if e_planes[0] <= x <= e_planes[1]:
                self.e_plane(x)

    def long_sweep(self, h_planes, e_planes):
        lo, hi = max(h_planes[0], e_planes[0]), min(h_planes[1], e_planes[1])
        for x in range(h_planes[0], lo):
            self.h_plane(x)

        def body(x, _):
            self.h_plane(x)
            self.e_plane(x)
            return 0

        lax.fori_loop(lo, hi + 1, body, 0)
        for x in range(hi + 1, e_planes[1] + 1):
            self.e_plane(x)


def copy_all(pairs, sems):
    copies = [pltpu.make_async_copy(a, b, sems.at[k]) for k, (a, b) in enumerate(pairs)]
    for copy in copies:
        copy.start()
    return copies


def load_and_pack(e, h, p, mat, via, fill, perm, cond, stre, rlx, ex, hx, px, cx, fx, out_c, out_d, out_a, out_b, sems):
    own, rows = pl.ds(LOW, NX), pl.ds(R0, NY)
    pairs = [(e, ex.at[:, own, rows]), (h, hx.at[:, own, rows]), (p, px.at[:, own, rows])]
    pairs += [(mat, cx.at[0, own, rows]), (via, cx.at[1, own, rows]), (fill, fx.at[0, own, rows])]
    copies = copy_all(pairs, sems)
    mats = materials(perm, cond, stre, rlx)
    for copy in copies:
        copy.wait()
    refs = {"e": ex, "h": hx, "p": px, "c": cx, "f": fx}
    low = tile_iota(0) < 4
    gy_odd, gx_odd = lax.axis_index("gy") % 2, lax.axis_index("gx") % 2

    def strip(x, r, out, upward):
        tiles = [refs[n][c, x + LOW, r:r + 8].astype(F32) for n, c in ORDER]
        for k in range(6):
            a, b = tiles[2 * k], tiles[2 * k + 1]
            if upward:
                out[k, x] = jnp.where(low, pltpu.roll(a, 4, 0), b)
            else:
                out[k, x] = jnp.where(low, a, pltpu.roll(b, 4, 0))

    def strips(up, down):
        def body(x, _):
            strip(x, RH - 8, up, True)
            strip(x, R0, down, False)
            return 0

        lax.fori_loop(0, NX, body, 0, unroll=2)

    @pl.when(gy_odd == 0)
    def _():
        strips(out_c, out_d)

    @pl.when(gy_odd == 1)
    def _():
        strips(out_d, out_c)

    own_rows = slice(R0, RH)

    def slab(out, d1, d2):
        for c in range(3):
            out[c] = ex[c, d1, own_rows]
            out[3 + c] = px[c, d1, own_rows]
            out[15 + c] = hx[c, d1, own_rows]
        for k, i in ((6, d1), (9, d2)):
            out[k] = cx[0, i, own_rows].astype(F32)
            out[k + 1] = cx[1, i, own_rows].astype(F32)
            out[k + 2] = fx[0, i, own_rows]
        for t in range(NY // 8):
            r = slice(R0 + 8 * t, R0 + 8 * t + 8)
            m = cx[0, d2, r]
            kp, bp = pick(mats, m, 2), pick(mats, m, 3)
            for c in range(3):
                out[12 + c, 8 * t:8 * t + 8] = kp * px[c, d2, r] + bp * ex[c, d2, r]

    @pl.when(gx_odd == 0)
    def _():
        slab(out_a, LOW + NX - 1, LOW + NX - 2)
        slab(out_b, LOW, LOW + 1)

    @pl.when(gx_odd == 1)
    def _():
        slab(out_b, LOW + NX - 1, LOW + NX - 2)
        slab(out_a, LOW, LOW + 1)


def first_edges(row_c, row_d, perm, cond, stre, rlx, conf, *refs):
    ex, hx, px, cx, fx, w, out_a, out_b = refs[5:]
    b = Block(ex, hx, px, cx, fx, w)
    b.masks()
    named = {"e": ex, "h": hx, "p": px, "c": cx, "f": fx}
    low = tile_iota(0) < 4
    gy_odd, gx_odd = lax.axis_index("gy") % 2, lax.axis_index("gx") % 2

    def rows_body(x, above_ref, below_ref):
        for k in range(6):
            above, below = above_ref[k, x], below_ref[k, x]
            both = (jnp.where(low, above, pltpu.roll(below, 4, 0)), jnp.where(low, pltpu.roll(above, 4, 0), below))
            for (n, c), tile in zip(ORDER[2 * k:2 * k + 2], both):
                named[n][c, x + LOW, RH:RE] = tile.astype(jnp.int32) if n == "c" else tile
        for c in (0, 2):
            ex[c, x + LOW, RE:RE + 1] = ex[c, x + LOW, R0:R0 + 1]
            hx[c, x + LOW, R0 - 1:R0] = hx[c, x + LOW, RE - 1:RE]

    def all_rows(above_ref, below_ref):
        def body(x, _):
            rows_body(x, above_ref, below_ref)
            return 0

        lax.fori_loop(0, NX, body, 0, unroll=2)

    @pl.when(gy_odd == 0)
    def _():
        all_rows(row_c, row_d)

    @pl.when(gy_odd == 1)
    def _():
        all_rows(row_d, row_c)

    mats, tables = materials(perm, cond, stre, rlx), via_tables(conf)
    for x in (1, 2, NX - 3, NX - 2):
        b.coef(x, mats, tables)
    b.h_plane(0)
    for x in (1, 2):
        b.h_plane(x)
        b.e_plane(x)
    b.h_plane(1)
    b.h_plane(NX - 4)
    for x in (NX - 3, NX - 2):
        b.h_plane(x)
        b.e_plane(x)
    b.h_plane(NX - 3)

    n = RE - R0

    def message(out, upward):
        d1, d2, d3 = (LOW + NX - 1, LOW + NX - 2, LOW + NX - 3) if upward else (LOW, LOW + 1, None)
        if upward:
            planes = [(hx, c, d2) for c in range(3)] + [(ex, c, d2) for c in range(3)] + [(hx, c, d3) for c in (1, 2)]
        else:
            planes = [(hx, c, d1) for c in range(3)] + [(hx, c, d2) for c in range(3)] + [(ex, c, d2) for c in (1, 2)]
        for k, (ref, c, i) in enumerate(planes):
            out[n * k:n * k + n] = ref[c, i, R0:RE]
        tiles = [(ex, c, d1) for c in range(3)] + [(px, c, d1) for c in range(3)]
        for i in (d1, d2):
            tiles += [(cx, 0, i), (cx, 1, i), (fx, 0, i)]
        tiles += [(px, c, d2) for c in range(3)] + [(hx, c, d1) for c in range(3)]
        for k, (ref, c, i) in enumerate(tiles):
            at = MSG2 * n + 8 * k
            out[at:at + 8] = ref[c, i, RH:RE].astype(F32)

    @pl.when(gx_odd == 0)
    def _():
        message(out_a, True)
        message(out_b, False)

    @pl.when(gx_odd == 1)
    def _():
        message(out_b, True)
        message(out_a, False)


def interior(cx, fx, perm, cond, stre, rlx, conf, *refs):
    ex, hx, px, w = refs[4:]
    b = Block(ex, hx, px, cx, fx, w)
    b.masks()
    mats, tables = materials(perm, cond, stre, rlx), via_tables(conf)
    b.coef(0, mats, tables)
    b.coef(NX - 1, mats, tables)

    def body(x, _):
        b.coef(x, mats, tables)
        return 0

    lax.fori_loop(3, NX - 3, body, 0)
    b.long_sweep((3, NX - 5), (3, NX - 4))
    b.long_sweep((2, NX - 4), (2, NX - 3))
    b.long_sweep((2, NX - 4), (3, NX - 4))
    b.long_sweep((3, NX - 5), (4, NX - 5))


def last_edges(got1_a, got1_b, got2_a, got2_b, perm, cond, stre, rlx, conf, *refs):
    e_out, h_out, p_out, ex, hx, px, cx, fx, w, sems = refs[6:]
    b = Block(ex, hx, px, cx, fx, w)
    b.masks()
    rows = pl.ds(R0, NY)
    outs = ((ex, e_out), (hx, h_out), (px, p_out))

    def part(first, count):
        return [(src.at[:, pl.ds(LOW + first, count), rows], dst.at[:, pl.ds(first, count)]) for src, dst in outs]

    done = copy_all(part(4, NX - 8), sems.at[pl.ds(0, 3)])
    gx_odd = lax.axis_index("gx") % 2
    n = RE - R0
    own_rows, halo_rows = slice(R0, RH), slice(RH, RE)

    def take(m1, m2, below):
        d1, d2, d3 = (LOW - 1, LOW - 2, LOW - 3) if below else (LOW + NX, LOW + NX + 1, None)

        def put(ref, c, i, k):
            at = MSG2 * n + 8 * k
            head, tail = m1[k], m2[at:at + 8]
            if ref is cx:
                head, tail = head.astype(jnp.int32), tail.astype(jnp.int32)
            ref[c, i, own_rows] = head
            ref[c, i, halo_rows] = tail

        for c in range(3):
            put(ex, c, d1, c)
            put(px, c, d1, 3 + c)
            put(px, c, d2, 12 + c)
            if below:
                put(hx, c, d1, 15 + c)
        for k, i in ((6, d1), (9, d2)):
            put(cx, 0, i, k)
            put(cx, 1, i, k + 1)
            put(fx, 0, i, k + 2)
        if below:
            planes = [(hx, c, d2) for c in range(3)] + [(ex, c, d2) for c in range(3)] + [(hx, c, d3) for c in (1, 2)]
        else:
            planes = [(hx, c, d1) for c in range(3)] + [(hx, c, d2) for c in range(3)] + [(ex, c, d2) for c in (1, 2)]
        for k, (ref, c, i) in enumerate(planes):
            ref[c, i, R0:RE] = m2[n * k:n * k + n]
        for i in (d1, d2):
            for c in (0, 2):
                ex[c, i, RE:RE + 1] = ex[c, i, R0:R0 + 1]
                hx[c, i, R0 - 1:R0] = hx[c, i, RE - 1:RE]

    @pl.when(gx_odd == 0)
    def _():
        take(got1_a, got2_a, False)
        take(got1_b, got2_b, True)

    @pl.when(gx_odd == 1)
    def _():
        take(got1_b, got2_b, False)
        take(got1_a, got2_a, True)

    mats, tables = materials(perm, cond, stre, rlx), via_tables(conf)
    for x in (-2, -1, NX, NX + 1):
        b.coef(x, mats, tables)
    m = NX - 16
    b.sweep((-1, -1), (-1, 0))
    b.sweep((-2, 0), (-2, 1))
    b.sweep((-2, 1), (-1, 2))
    b.sweep((-1, 2), (0, 3))
    for copy in done:
        copy.wait()
    done = copy_all(part(0, 4), sems.at[pl.ds(0, 3)])
    b.sweep((m + 15, m + 15), (m + 15, m + 16))
    b.sweep((m + 14, m + 16), (m + 14, m + 17))
    b.sweep((m + 13, m + 16), (m + 13, m + 16))
    b.sweep((m + 12, m + 15), (m + 12, m + 15))
    done += copy_all(part(NX - 4, 4), sems.at[pl.ds(3, 3)])
    for copy in done:
        copy.wait()


def shards(efield, hfield, polar, material_map, via_index, fill_fraction, permittivity, conductivity, debye_strength, relax_time, conformal):
    vmem = pl.BlockSpec(memory_space=pltpu.VMEM)
    smem = pl.BlockSpec(memory_space=pltpu.SMEM)
    hbm = pl.BlockSpec(memory_space=pltpu.HBM)
    conformal = conformal.T
    cells = (efield, hfield, polar, material_map, via_index, fill_fraction)
    cells = tuple(pltpu.with_memory_space_constraint(a, pltpu.HBM) for a in cells)
    tables = (permittivity, conductivity, debye_strength, relax_time)
    tables = tuple(pltpu.with_memory_space_constraint(a, pltpu.HBM) for a in tables)
    shape = jax.ShapeDtypeStruct
    field, slab1 = shape((3,) + EXT, F32), shape((MSG1, NY, NZ), F32)
    slab2, strip = shape((MSG2_ROWS, NZ), F32), shape((6, NX, 8, NZ), F32)
    ints, fill, coef = shape((2,) + EXT, jnp.int32), shape((1,) + EXT, F32), shape((7,) + EXT, F32)
    result = shape((3, NX, NY, NZ), F32)
    params = pltpu.CompilerParams(vmem_limit_bytes=4 << 20)

    ex, hx, px, cx, fx, strip_c, strip_d, slab_a, slab_b = pl.pallas_call(
        load_and_pack, out_shape=(field, field, field, ints, fill, strip, strip, slab1, slab1),
        in_specs=[hbm] * 6 + [smem] * 4, out_specs=(vmem,) * 9,
        scratch_shapes=[pltpu.SemaphoreType.DMA((6,))], compiler_params=params, name="load_and_pack",
    )(*cells, *tables)
    row_c = swapped(strip_c, "gy", 0)
    row_d = swapped(strip_d, "gy", 1)
    got1_b = swapped(slab_b, "gx", 1)
    got1_a = swapped(slab_a, "gx", 0)
    ex, hx, px, cx, fx, w, edge_a, edge_b = pl.pallas_call(
        first_edges, out_shape=(field, field, field, ints, fill, coef, slab2, slab2),
        in_specs=[vmem] * 2 + [smem] * 5 + [vmem] * 5, out_specs=(vmem,) * 8,
        input_output_aliases={7 + k: k for k in range(5)}, compiler_params=params, name="first_edges",
    )(row_c, row_d, *tables, conformal, ex, hx, px, cx, fx)
    got2_b = swapped(edge_b, "gx", 1)
    got2_a = swapped(edge_a, "gx", 0)
    ex, hx, px, w = pl.pallas_call(
        interior, out_shape=(field, field, field, coef),
        in_specs=[vmem] * 2 + [smem] * 5 + [vmem] * 4, out_specs=(vmem,) * 4,
        input_output_aliases={7 + k: k for k in range(4)}, compiler_params=params, name="interior",
        cost_estimate=pl.CostEstimate(flops=80_000_000, bytes_accessed=20_000_000, transcendentals=0),
    )(cx, fx, *tables, conformal, ex, hx, px, w)
    outs = pl.pallas_call(
        last_edges, out_shape=(result,) * 3 + (field, field, field, ints, fill, coef),
        in_specs=[vmem] * 4 + [smem] * 5 + [vmem] * 6, out_specs=(hbm,) * 3 + (vmem,) * 6,
        input_output_aliases={9 + k: 3 + k for k in range(6)},
        scratch_shapes=[pltpu.SemaphoreType.DMA((6,))], compiler_params=params, name="last_edges",
    )(got1_a, got1_b, got2_a, got2_b, *tables, conformal, ex, hx, px, cx, fx, w)
    return outs[:3]


def solution(mesh):
    whole, cell = P(None, "gx", "gy", None), P("gx", "gy", None)
    return jax.shard_map(
        shards, mesh=mesh, in_specs=(whole,) * 3 + (cell,) * 3 + (P(),) * 5, out_specs=(whole,) * 3, check_vma=False,
    )
```

```python
import jax
import jax.numpy as jnp
from jax import lax
from jax.experimental import pallas as pl
from jax.experimental.pallas import tpu as pltpu
from jax.sharding import PartitionSpec as P

DT = 0.55
F32 = jnp.float32

NX, NY, NZ = 16, 32, 128
LOW, HIGH = 3, 2
R0, RH, RE = 8, 8 + NY, 16 + NY
EXT = (NX + LOW + HIGH, RE + 8, NZ)
TILES = (RE - R0) // 8
OWN, HALO = range(TILES - 1), range(TILES - 1, TILES)
MSG1, MSG2 = 18, 8
MSG2_ROWS = MSG2 * (RE - R0) + MSG1 * 8

ORDER = (("e", 0), ("e", 1), ("e", 2), ("h", 0), ("h", 1), ("h", 2), ("p", 0), ("p", 1), ("p", 2), ("f", 0), ("c", 0), ("c", 1))


def swapped(value, axis, first):
    pairs = []
    for low in range(first, lax.axis_size(axis) - 1, 2):
        pairs += [(low, low + 1), (low + 1, low)]
    return lax.ppermute(value, axis, pairs)


def tile_iota(dim):
    return lax.broadcasted_iota(jnp.int32, (8, NZ), dim)


def make_tables(perm, cond, stre, rlx, conf, tab):
    for m in range(3):
        tau = jnp.full((8, NZ), rlx[m], F32)
        inv = 1.0 / (2.0 * tau + DT)
        tab[5 * m] = jnp.full((8, NZ), perm[m], F32)
        tab[5 * m + 1] = jnp.full((8, NZ), cond[m] * (DT / 2), F32)
        tab[5 * m + 2] = (2.0 * tau - DT) * inv
        tab[5 * m + 3] = jnp.full((8, NZ), stre[m], F32) * (2.0 * DT) * inv
        tab[5 * m + 4] = 2.0 * DT * inv
    lane = tile_iota(1)
    for c in range(3):
        table = jnp.zeros((8, NZ), F32)
        for v in range(8):
            table = jnp.where(lane == v, conf[c, v], table)
        tab[15 + c] = table


def pick(tab, m, i):
    return jnp.where(m == 0, tab[i], jnp.where(m == 1, tab[5 + i], tab[10 + i]))


class Block:
    def __init__(self, ex, hx, px, cx, fx, w=None):
        self.e, self.h, self.p, self.c, self.f, self.w = ex, hx, px, cx, fx, w

    def masks(self):
        gy = lax.axis_index("gy")
        row = tile_iota(0)
        out = ((row < 4) & (gy == lax.axis_size("gy") - 1)) | ((row >= 4) & (gy == 0))
        self.row_in = jnp.where(out, 0.0, 1.0).astype(F32)
        lane = tile_iota(1)
        self.last, self.first = lane == NZ - 1, lane == 0

    def plane_in(self, x):
        if not isinstance(x, int) or 0 <= x < NX:
            return None
        gx = lax.axis_index("gx")
        out = gx == 0 if x < 0 else gx == lax.axis_size("gx") - 1
        return jnp.where(out, 0.0, 1.0).astype(F32)

    def zf(self, a):
        return jnp.where(self.last, 0.0, pltpu.roll(a, NZ - 1, 1))

    def zb(self, a):
        return jnp.where(self.first, 0.0, pltpu.roll(a, 1, 1))

    def coef(self, x, tab, tiles):
        i = x + LOW
        inside = self.plane_in(x)
        for t in tiles:
            r = slice(R0 + 8 * t, R0 + 8 * t + 8)
            m, v, f = self.c[0, i, r], self.c[1, i, r], self.f[0, i, r]
            pe, s, kp, bp, omk = (pick(tab, m, k) for k in range(5))
            eps = pe * (1.0 + f)
            inv = 1.0 / (eps + s)
            self.w[0, i, r] = (eps - s) * inv - inv * bp
            self.w[1, i, r] = inv * omk
            self.w[2, i, r] = kp
            self.w[3, i, r] = bp
            scale = inv * DT if inside is None else inv * (DT * inside)
            if t == TILES - 1:
                scale = scale * self.row_in
            for c in range(3):
                self.w[4 + c, i, r] = scale * jnp.take_along_axis(tab[15 + c], v, axis=1)

    def take_tiles(self, below, part, rows):
        d1, d2 = (LOW - 1, LOW - 2) if below else (LOW + NX, LOW + NX + 1)
        for c in range(3):
            self.e[c, d1, rows] = part(c)
            self.p[c, d1, rows] = part(3 + c)
            self.p[c, d2, rows] = part(12 + c)
            if below:
                self.h[c, d1, rows] = part(15 + c)
        for k, i in ((6, d1), (9, d2)):
            self.c[0, i, rows] = part(k).astype(jnp.int32)
            self.c[1, i, rows] = part(k + 1).astype(jnp.int32)
            self.f[0, i, rows] = part(k + 2)

    def h_plane(self, x):
        i = x + LOW
        e, h = self.e, self.h
        inside = self.plane_in(x)
        for t in range(TILES):
            a = R0 + 8 * t
            r, up = slice(a, a + 8), slice(a + 1, a + 9)
            e0, e1, e2 = e[0, i, r], e[1, i, r], e[2, i, r]
            m = DT if inside is None else DT * inside
            if t == TILES - 1:
                m = self.row_in * m
            h0 = h[0, i, r] - m * ((e[2, i, up] - e2) - (self.zf(e1) - e1))
            h1 = h[1, i, r] - m * ((self.zf(e0) - e0) - (e[2, i + 1, r] - e2))
            h2 = h[2, i, r] - m * ((e[1, i + 1, r] - e1) - (e[0, i, up] - e0))
            h[0, i, r], h[1, i, r], h[2, i, r] = h0, h1, h2
        h[0, i, R0 - 1:R0] = h0[7:8]
        h[2, i, R0 - 1:R0] = h2[7:8]

    def e_plane(self, x, tiles=range(TILES)):
        i = x + LOW
        e, h, p, w = self.e, self.h, self.p, self.w
        for t in tiles:
            a = R0 + 8 * t
            r, down = slice(a, a + 8), slice(a - 1, a + 7)
            h0, h1, h2 = h[0, i, r], h[1, i, r], h[2, i, r]
            curl = (
                (h2 - h[2, i, down]) - (h1 - self.zb(h1)),
                (h0 - self.zb(h0)) - (h2 - h[2, i - 1, r]),
                (h1 - h[1, i - 1, r]) - (h0 - h[0, i, down]),
            )
            w0, w1, w2, w3 = (w[k, i, r] for k in range(4))
            for c in range(3):
                ec, pc = e[c, i, r], p[c, i, r]
                new = w0 * ec + w1 * pc + w[4 + c, i, r] * curl[c]
                e[c, i, r] = new
                p[c, i, r] = w2 * pc + w3 * ec
                if t == 0 and c != 1 and len(tiles) == TILES:
                    e[c, i, RE:RE + 1] = new[0:1]

    def sweep(self, h_planes, e_planes, tiles=range(TILES)):
        for x in range(min(h_planes[0], e_planes[0]), max(h_planes[1], e_planes[1]) + 1):
            if h_planes[0] <= x <= h_planes[1]:
                self.h_plane(x)
            if e_planes[0] <= x <= e_planes[1]:
                self.e_plane(x, tiles)


def for_sides(take, from_a, from_b):
    odd = lax.axis_index("gx") % 2

    @pl.when(odd == 0)
    def _():
        take(*from_a, False)
        take(*from_b, True)

    @pl.when(odd == 1)
    def _():
        take(*from_b, False)
        take(*from_a, True)


def copy_all(pairs, sems):
    copies = [pltpu.make_async_copy(a, b, sems.at[k]) for k, (a, b) in enumerate(pairs)]
    for copy in copies:
        copy.start()
    return copies


def load_and_pack(e, h, p, mat, via, fill, perm, cond, stre, rlx, conf, ex, hx, px, cx, fx, tab, out_c, out_d, out_a, out_b, *scratch):
    smalls, sems = scratch[:5], scratch[5]
    own = pl.ds(LOW, NX)
    copies = []
    for at, n in ((0, 8), (NY - 8, 8), (8, NY - 16)):
        there, here = pl.ds(at, n), pl.ds(R0 + at, n)
        pairs = [(a.at[:, :, there], b.at[:, own, here]) for a, b in ((e, ex), (h, hx), (p, px))]
        pairs += [(a.at[:, there], b.at[k, own, here]) for a, b, k in ((mat, cx, 0), (via, cx, 1), (fill, fx, 0))]
        copies += copy_all(pairs, sems.at[pl.ds(len(copies), 6)])
    few = copy_all(zip((perm, cond, stre, rlx, conf), smalls), sems.at[pl.ds(18, 5)])
    for copy in few:
        copy.wait()
    make_tables(*smalls, tab)
    for copy in copies[:12]:
        copy.wait()
    refs = {"e": ex, "h": hx, "p": px, "c": cx, "f": fx}
    low = tile_iota(0) < 4
    gy_odd, gx_odd = lax.axis_index("gy") % 2, lax.axis_index("gx") % 2

    def strip(x, r, out, upward):
        tiles = [refs[n][c, x + LOW, r:r + 8].astype(F32) for n, c in ORDER]
        for k in range(6):
            a, b = tiles[2 * k], tiles[2 * k + 1]
            if upward:
                out[k, x] = jnp.where(low, pltpu.roll(a, 4, 0), b)
            else:
                out[k, x] = jnp.where(low, a, pltpu.roll(b, 4, 0))

    def strips(up, down):
        def body(x, _):
            strip(x, RH - 8, up, True)
            strip(x, R0, down, False)
            return 0

        lax.fori_loop(0, NX, body, 0, unroll=2)

    @pl.when(gy_odd == 0)
    def _():
        strips(out_c, out_d)

    @pl.when(gy_odd == 1)
    def _():
        strips(out_d, out_c)

    for copy in copies[12:]:
        copy.wait()
    own_rows = slice(R0, RH)

    def slab(out, d1, d2):
        for c in range(3):
            out[c] = ex[c, d1, own_rows]
            out[3 + c] = px[c, d1, own_rows]
            out[15 + c] = hx[c, d1, own_rows]
        for k, i in ((6, d1), (9, d2)):
            out[k] = cx[0, i, own_rows].astype(F32)
            out[k + 1] = cx[1, i, own_rows].astype(F32)
            out[k + 2] = fx[0, i, own_rows]
        for t in range(NY // 8):
            r = slice(R0 + 8 * t, R0 + 8 * t + 8)
            m = cx[0, d2, r]
            kp, bp = pick(tab, m, 2), pick(tab, m, 3)
            for c in range(3):
                out[12 + c, 8 * t:8 * t + 8] = kp * px[c, d2, r] + bp * ex[c, d2, r]

    @pl.when(gx_odd == 0)
    def _():
        slab(out_a, LOW + NX - 1, LOW + NX - 2)
        slab(out_b, LOW, LOW + 1)

    @pl.when(gx_odd == 1)
    def _():
        slab(out_b, LOW + NX - 1, LOW + NX - 2)
        slab(out_a, LOW, LOW + 1)


def own_coefs(cx, fx, tab, w):
    b = Block(None, None, None, cx, fx, w)

    def body(x, _):
        b.coef(x, tab, OWN)
        return 0

    lax.fori_loop(0, NX, body, 0, unroll=2)


def first_edges(row_c, row_d, tab, *refs):
    ex, hx, px, cx, fx, w, out_a, out_b = refs[6:]
    b = Block(ex, hx, px, cx, fx, w)
    b.masks()
    named = {"e": ex, "h": hx, "p": px, "c": cx, "f": fx}
    low = tile_iota(0) < 4
    gy_odd, gx_odd = lax.axis_index("gy") % 2, lax.axis_index("gx") % 2

    def rows_body(x, above_ref, below_ref):
        for k in range(6):
            above, below = above_ref[k, x], below_ref[k, x]
            both = (jnp.where(low, above, pltpu.roll(below, 4, 0)), jnp.where(low, pltpu.roll(above, 4, 0), below))
            for (n, c), tile in zip(ORDER[2 * k:2 * k + 2], both):
                named[n][c, x + LOW, RH:RE] = tile.astype(jnp.int32) if n == "c" else tile
        for c in (0, 2):
            ex[c, x + LOW, RE:RE + 1] = ex[c, x + LOW, R0:R0 + 1]
            hx[c, x + LOW, R0 - 1:R0] = hx[c, x + LOW, RE - 1:RE]

    def all_rows(above_ref, below_ref):
        def body(x, _):
            rows_body(x, above_ref, below_ref)
            return 0

        lax.fori_loop(0, NX, body, 0, unroll=2)

    @pl.when(gy_odd == 0)
    def _():
        all_rows(row_c, row_d)

    @pl.when(gy_odd == 1)
    def _():
        all_rows(row_d, row_c)

    for x in (1, 2, NX - 3, NX - 2):
        b.coef(x, tab, HALO)
    b.h_plane(0)
    for x in (1, 2):
        b.h_plane(x)
        b.e_plane(x)
    b.h_plane(1)
    b.h_plane(NX - 4)
    for x in (NX - 3, NX - 2):
        b.h_plane(x)
        b.e_plane(x)
    b.h_plane(NX - 3)

    n = RE - R0

    def message(out, upward):
        d1, d2, d3 = (LOW + NX - 1, LOW + NX - 2, LOW + NX - 3) if upward else (LOW, LOW + 1, None)
        if upward:
            planes = [(hx, c, d2) for c in range(3)] + [(ex, c, d2) for c in range(3)] + [(hx, c, d3) for c in (1, 2)]
        else:
            planes = [(hx, c, d1) for c in range(3)] + [(hx, c, d2) for c in range(3)] + [(ex, c, d2) for c in (1, 2)]
        for k, (ref, c, i) in enumerate(planes):
            out[n * k:n * k + n] = ref[c, i, R0:RE]
        tiles = [(ex, c, d1) for c in range(3)] + [(px, c, d1) for c in range(3)]
        for i in (d1, d2):
            tiles += [(cx, 0, i), (cx, 1, i), (fx, 0, i)]
        tiles += [(px, c, d2) for c in range(3)] + [(hx, c, d1) for c in range(3)]
        for k, (ref, c, i) in enumerate(tiles):
            at = MSG2 * n + 8 * k
            out[at:at + 8] = ref[c, i, RH:RE].astype(F32)

    @pl.when(gx_odd == 0)
    def _():
        message(out_a, True)
        message(out_b, False)

    @pl.when(gx_odd == 1)
    def _():
        message(out_b, True)
        message(out_a, False)


def interior(cx, fx, tab, *refs):
    ex, hx, px, w = refs[4:]
    b = Block(ex, hx, px, cx, fx, w)
    b.masks()
    for x in (0, *range(3, NX - 3), NX - 1):
        b.coef(x, tab, HALO)
    b.sweep((3, NX - 5), (3, NX - 4))
    b.sweep((2, NX - 4), (2, NX - 3))
    b.sweep((2, NX - 4), (3, NX - 4))
    b.sweep((3, NX - 5), (4, NX - 5), OWN)


def neighbour_cells(got1_a, got1_b, tab, *refs):
    ex, hx, px, cx, fx, w = refs[6:]
    b = Block(ex, hx, px, cx, fx, w)

    def take(m1, below):
        b.take_tiles(below, lambda k: m1[k], slice(R0, RH))

    for_sides(take, (got1_a,), (got1_b,))
    for x in (-2, -1, NX, NX + 1):
        b.coef(x, tab, OWN)


def last_edges(got2_a, got2_b, tab, *refs):
    e_out, h_out, p_out, ex, hx, px, cx, fx, w, sems = refs[6:]
    b = Block(ex, hx, px, cx, fx, w)
    b.masks()
    rows = pl.ds(R0, NY)
    done = []

    def store(first, count):
        pairs = []
        for src, dst in ((ex, e_out), (hx, h_out), (px, p_out)):
            pairs.append((src.at[:, pl.ds(LOW + first, count), rows], dst.at[:, pl.ds(first, count)]))
        done.extend(copy_all(pairs, sems.at[pl.ds(len(done), 3)]))

    store(4, NX - 8)
    n = RE - R0

    def take(m2, below):
        at = MSG2 * n
        b.take_tiles(below, lambda k: m2[at + 8 * k:at + 8 * k + 8], slice(RH, RE))
        d1, d2, d3 = (LOW - 1, LOW - 2, LOW - 3) if below else (LOW + NX, LOW + NX + 1, None)
        if below:
            planes = [(hx, c, d2) for c in range(3)] + [(ex, c, d2) for c in range(3)] + [(hx, c, d3) for c in (1, 2)]
        else:
            planes = [(hx, c, d1) for c in range(3)] + [(hx, c, d2) for c in range(3)] + [(ex, c, d2) for c in (1, 2)]
        for k, (ref, c, i) in enumerate(planes):
            ref[c, i, R0:RE] = m2[n * k:n * k + n]
        for i in (d1, d2):
            for c in (0, 2):
                ex[c, i, RE:RE + 1] = ex[c, i, R0:R0 + 1]
                hx[c, i, R0 - 1:R0] = hx[c, i, RE - 1:RE]

    for_sides(take, (got2_a,), (got2_b,))
    for x in (-2, -1, NX, NX + 1):
        b.coef(x, tab, HALO)
    b.sweep((-1, -1), (-1, 0))
    b.sweep((-2, 0), (-2, 1))
    b.sweep((-2, 1), (-1, 2))
    b.sweep((-1, 2), (0, 3), OWN)
    store(0, 4)
    b.sweep((NX - 1, NX - 1), (NX - 1, NX))
    b.sweep((NX - 2, NX), (NX - 2, NX + 1))
    b.sweep((NX - 3, NX), (NX - 3, NX))
    b.sweep((NX - 4, NX - 1), (NX - 4, NX - 1), OWN)
    store(NX - 4, 4)
    for copy in done:
        copy.wait()


def shards(efield, hfield, polar, material_map, via_index, fill_fraction, permittivity, conductivity, debye_strength, relax_time, conformal):
    vmem = pl.BlockSpec(memory_space=pltpu.VMEM)
    hbm = pl.BlockSpec(memory_space=pltpu.HBM)
    conformal = conformal.T
    cells = (efield, hfield, polar, material_map, via_index, fill_fraction)
    cells = tuple(pltpu.with_memory_space_constraint(a, pltpu.HBM) for a in cells)
    tables = (permittivity, conductivity, debye_strength, relax_time, conformal)
    tables = tuple(pltpu.with_memory_space_constraint(a, pltpu.HBM) for a in tables)
    shape = jax.ShapeDtypeStruct
    field, slab1 = shape((3,) + EXT, F32), shape((MSG1, NY, NZ), F32)
    slab2, strip = shape((MSG2_ROWS, NZ), F32), shape((6, NX, 8, NZ), F32)
    ints, fill, coef = shape((2,) + EXT, jnp.int32), shape((1,) + EXT, F32), shape((7,) + EXT, F32)
    result = shape((3, NX, NY, NZ), F32)
    params = pltpu.CompilerParams(vmem_limit_bytes=4 << 20)

    ex, hx, px, cx, fx, tab, strip_c, strip_d, slab_a, slab_b = pl.pallas_call(
        load_and_pack, out_shape=(field, field, field, ints, fill, shape((18, 8, NZ), F32), strip, strip, slab1, slab1),
        in_specs=[hbm] * 11, out_specs=(vmem,) * 10,
        scratch_shapes=[pltpu.SMEM((3,), F32)] * 4 + [pltpu.SMEM((3, 8), F32), pltpu.SemaphoreType.DMA((23,))],
        compiler_params=params, name="load_and_pack",
    )(*cells, *tables)
    row_c = swapped(strip_c, "gy", 0)
    row_d = swapped(strip_d, "gy", 1)
    got1_a = swapped(slab_a, "gx", 0)
    got1_b = swapped(slab_b, "gx", 1)
    w = pl.pallas_call(
        own_coefs, out_shape=coef, in_specs=[vmem] * 3, out_specs=vmem, compiler_params=params, name="own_coefs",
        cost_estimate=pl.CostEstimate(flops=10_000_000, bytes_accessed=4_000_000, transcendentals=0),
    )(cx, fx, tab)
    ex, hx, px, cx, fx, w, send_a, send_b = pl.pallas_call(
        first_edges, out_shape=(field, field, field, ints, fill, coef, slab2, slab2),
        in_specs=[vmem] * 9, out_specs=(vmem,) * 8,
        input_output_aliases={3 + k: k for k in range(6)}, compiler_params=params, name="first_edges",
    )(row_c, row_d, tab, ex, hx, px, cx, fx, w)
    got2_a = swapped(send_a, "gx", 0)
    got2_b = swapped(send_b, "gx", 1)
    ex, hx, px, w = pl.pallas_call(
        interior, out_shape=(field, field, field, coef),
        in_specs=[vmem] * 7, out_specs=(vmem,) * 4,
        input_output_aliases={3 + k: k for k in range(4)}, compiler_params=params, name="interior",
        cost_estimate=pl.CostEstimate(flops=80_000_000, bytes_accessed=20_000_000, transcendentals=0),
    )(cx, fx, tab, ex, hx, px, w)
    state = (ex, hx, px, cx, fx, w)
    shapes = (field, field, field, ints, fill, coef)
    state = pl.pallas_call(
        neighbour_cells, out_shape=shapes, in_specs=[vmem] * 9, out_specs=(vmem,) * 6,
        input_output_aliases={3 + k: k for k in range(6)}, compiler_params=params, name="neighbour_cells",
    )(got1_a, got1_b, tab, *state)
    outs = pl.pallas_call(
        last_edges, out_shape=(result,) * 3 + shapes, in_specs=[vmem] * 9, out_specs=(hbm,) * 3 + (vmem,) * 6,
        input_output_aliases={3 + k: 3 + k for k in range(6)},
        scratch_shapes=[pltpu.SemaphoreType.DMA((9,))], compiler_params=params, name="last_edges",
    )(got2_a, got2_b, tab, *state)
    return outs[:3]


def solution(mesh):
    whole, cell = P(None, "gx", "gy", None), P("gx", "gy", None)

    return jax.shard_map(
        shards, mesh=mesh, in_specs=(whole,) * 3 + (cell,) * 3 + (P(),) * 5, out_specs=(whole,) * 3, check_vma=False,
    )
```

```python
import jax
import jax.numpy as jnp
from jax import lax
from jax.experimental import pallas as pl
from jax.experimental.pallas import tpu as pltpu
from jax.sharding import PartitionSpec as P

DT = 0.55
F32 = jnp.float32

NX, NY, NZ = 16, 32, 128
LOW, HIGH = 3, 2
R0, RH, RE = 8, 8 + NY, 16 + NY
EXT = (NX + LOW + HIGH, RE + 8, NZ)
TILES = (RE - R0) // 8
OWN, HALO = range(TILES - 1), range(TILES - 1, TILES)
MSG1, MSG2 = 18, 8
MSG2_ROWS = MSG2 * (RE - R0) + MSG1 * 8

ORDER = (("e", 0), ("e", 1), ("e", 2), ("h", 0), ("h", 1), ("h", 2), ("p", 0), ("p", 1), ("p", 2), ("f", 0), ("c", 0), ("c", 1))


def swapped(value, axis, first):
    pairs = []
    for low in range(first, lax.axis_size(axis) - 1, 2):
        pairs += [(low, low + 1), (low + 1, low)]
    return lax.ppermute(value, axis, pairs)


def tile_iota(dim):
    return lax.broadcasted_iota(jnp.int32, (8, NZ), dim)


def make_tables(perm, cond, stre, rlx, conf, tab):
    for m in range(3):
        tau = jnp.full((8, NZ), rlx[m], F32)
        inv = 1.0 / (2.0 * tau + DT)
        tab[5 * m] = jnp.full((8, NZ), perm[m], F32)
        tab[5 * m + 1] = jnp.full((8, NZ), cond[m] * (DT / 2), F32)
        tab[5 * m + 2] = (2.0 * tau - DT) * inv
        tab[5 * m + 3] = jnp.full((8, NZ), stre[m], F32) * (2.0 * DT) * inv
        tab[5 * m + 4] = 2.0 * DT * inv
    lane = tile_iota(1)
    for c in range(3):
        table = jnp.zeros((8, NZ), F32)
        for v in range(8):
            table = jnp.where(lane == v, conf[c, v], table)
        tab[15 + c] = table


def pick(tab, m, i):
    return jnp.where(m == 0, tab[i], jnp.where(m == 1, tab[5 + i], tab[10 + i]))


class Block:
    def __init__(self, ex, hx, px, cx, fx, w=None):
        self.e, self.h, self.p, self.c, self.f, self.w = ex, hx, px, cx, fx, w

    def masks(self):
        gy = lax.axis_index("gy")
        row = tile_iota(0)
        out = ((row < 4) & (gy == lax.axis_size("gy") - 1)) | ((row >= 4) & (gy == 0))
        self.row_in = jnp.where(out, 0.0, 1.0).astype(F32)
        lane = tile_iota(1)
        self.last, self.first = lane == NZ - 1, lane == 0

    def plane_in(self, x):
        if not isinstance(x, int) or 0 <= x < NX:
            return None
        gx = lax.axis_index("gx")
        out = gx == 0 if x < 0 else gx == lax.axis_size("gx") - 1
        return jnp.where(out, 0.0, 1.0).astype(F32)

    def zf(self, a):
        return jnp.where(self.last, 0.0, pltpu.roll(a, NZ - 1, 1))

    def zb(self, a):
        return jnp.where(self.first, 0.0, pltpu.roll(a, 1, 1))

    def coef(self, x, tab, tiles):
        i = x + LOW
        inside = self.plane_in(x)
        for t in tiles:
            r = slice(R0 + 8 * t, R0 + 8 * t + 8)
            m, v, f = self.c[0, i, r], self.c[1, i, r], self.f[0, i, r]
            pe, s, kp, bp, omk = (pick(tab, m, k) for k in range(5))
            eps = pe * (1.0 + f)
            inv = 1.0 / (eps + s)
            self.w[0, i, r] = (eps - s) * inv - inv * bp
            self.w[1, i, r] = inv * omk
            self.w[2, i, r] = kp
            self.w[3, i, r] = bp
            scale = inv * DT if inside is None else inv * (DT * inside)
            if t == TILES - 1:
                scale = scale * self.row_in
            for c in range(3):
                self.w[4 + c, i, r] = scale * jnp.take_along_axis(tab[15 + c], v, axis=1)

    def take_tiles(self, below, part, rows):
        d1, d2 = (LOW - 1, LOW - 2) if below else (LOW + NX, LOW + NX + 1)
        for c in range(3):
            self.e[c, d1, rows] = part(c)
            self.p[c, d1, rows] = part(3 + c)
            self.p[c, d2, rows] = part(12 + c)
            if below:
                self.h[c, d1, rows] = part(15 + c)
        for k, i in ((6, d1), (9, d2)):
            self.c[0, i, rows] = part(k).astype(jnp.int32)
            self.c[1, i, rows] = part(k + 1).astype(jnp.int32)
            self.f[0, i, rows] = part(k + 2)

    def h_plane(self, x):
        i = x + LOW
        e, h = self.e, self.h
        inside = self.plane_in(x)
        for t in range(TILES):
            a = R0 + 8 * t
            r, up = slice(a, a + 8), slice(a + 1, a + 9)
            e0, e1, e2 = e[0, i, r], e[1, i, r], e[2, i, r]
            m = DT if inside is None else DT * inside
            if t == TILES - 1:
                m = self.row_in * m
            h0 = h[0, i, r] - m * ((e[2, i, up] - e2) - (self.zf(e1) - e1))
            h1 = h[1, i, r] - m * ((self.zf(e0) - e0) - (e[2, i + 1, r] - e2))
            h2 = h[2, i, r] - m * ((e[1, i + 1, r] - e1) - (e[0, i, up] - e0))
            h[0, i, r], h[1, i, r], h[2, i, r] = h0, h1, h2
        h[0, i, R0 - 1:R0] = h0[7:8]
        h[2, i, R0 - 1:R0] = h2[7:8]

    def e_plane(self, x, tiles=range(TILES)):
        i = x + LOW
        e, h, p, w = self.e, self.h, self.p, self.w
        for t in tiles:
            a = R0 + 8 * t
            r, down = slice(a, a + 8), slice(a - 1, a + 7)
            h0, h1, h2 = h[0, i, r], h[1, i, r], h[2, i, r]
            curl = (
                (h2 - h[2, i, down]) - (h1 - self.zb(h1)),
                (h0 - self.zb(h0)) - (h2 - h[2, i - 1, r]),
                (h1 - h[1, i - 1, r]) - (h0 - h[0, i, down]),
            )
            w0, w1, w2, w3 = (w[k, i, r] for k in range(4))
            for c in range(3):
                ec, pc = e[c, i, r], p[c, i, r]
                new = w0 * ec + w1 * pc + w[4 + c, i, r] * curl[c]
                e[c, i, r] = new
                p[c, i, r] = w2 * pc + w3 * ec
                if t == 0 and c != 1 and len(tiles) == TILES:
                    e[c, i, RE:RE + 1] = new[0:1]

    def sweep(self, h_planes, e_planes, tiles=range(TILES)):
        for x in range(min(h_planes[0], e_planes[0]), max(h_planes[1], e_planes[1]) + 1):
            if h_planes[0] <= x <= h_planes[1]:
                self.h_plane(x)
            if e_planes[0] <= x <= e_planes[1]:
                self.e_plane(x, tiles)


def for_sides(take, from_a, from_b):
    odd = lax.axis_index("gx") % 2

    @pl.when(odd == 0)
    def _():
        take(*from_a, False)
        take(*from_b, True)

    @pl.when(odd == 1)
    def _():
        take(*from_b, False)
        take(*from_a, True)


def copy_all(pairs, sems):
    copies = [pltpu.make_async_copy(a, b, sems.at[k]) for k, (a, b) in enumerate(pairs)]
    for copy in copies:
        copy.start()
    return copies


LATE = (8, NY - 16)


def load_pairs(at, n, arrays, refs, first, count):
    e, h, p, mat, via, fill = arrays
    ex, hx, px, cx, fx = refs
    planes, there = pl.ds(first, count), pl.ds(at, n)
    dst, here = pl.ds(LOW + first, count), pl.ds(R0 + at, n)
    pairs = [(a.at[:, planes, there], b.at[:, dst, here]) for a, b in ((e, ex), (h, hx), (p, px))]
    return pairs + [(a.at[planes, there], b.at[k, dst, here]) for a, b, k in ((mat, cx, 0), (via, cx, 1), (fill, fx, 0))]


def load_and_pack(e, h, p, mat, via, fill, perm, cond, stre, rlx, conf, ex, hx, px, cx, fx, tab, out_c, out_d, out_a, out_b, *scratch):
    smalls, sems = scratch[:5], scratch[5]
    copies = []
    refs = (e, h, p, mat, via, fill), (ex, hx, px, cx, fx)
    for at in (0, NY - 8):
        copies += copy_all(load_pairs(at, 8, *refs, 0, NX), sems.at[pl.ds(len(copies), 6)])
    for first in (0, NX - 2):
        copies += copy_all(load_pairs(*LATE, *refs, first, 2), sems.at[pl.ds(len(copies), 6)])
    few = copy_all(zip((perm, cond, stre, rlx, conf), smalls), sems.at[pl.ds(24, 5)])
    for copy in few:
        copy.wait()
    make_tables(*smalls, tab)
    for copy in copies[:12]:
        copy.wait()
    refs = {"e": ex, "h": hx, "p": px, "c": cx, "f": fx}
    low = tile_iota(0) < 4
    gy_odd, gx_odd = lax.axis_index("gy") % 2, lax.axis_index("gx") % 2

    def strip(x, r, out, upward):
        tiles = [refs[n][c, x + LOW, r:r + 8].astype(F32) for n, c in ORDER]
        for k in range(6):
            a, b = tiles[2 * k], tiles[2 * k + 1]
            if upward:
                out[k, x] = jnp.where(low, pltpu.roll(a, 4, 0), b)
            else:
                out[k, x] = jnp.where(low, a, pltpu.roll(b, 4, 0))

    def strips(up, down):
        def body(x, _):
            strip(x, RH - 8, up, True)
            strip(x, R0, down, False)
            return 0

        lax.fori_loop(0, NX, body, 0, unroll=2)

    @pl.when(gy_odd == 0)
    def _():
        strips(out_c, out_d)

    @pl.when(gy_odd == 1)
    def _():
        strips(out_d, out_c)

    for copy in copies[12:]:
        copy.wait()
    own_rows = slice(R0, RH)

    def slab(out, d1, d2):
        for c in range(3):
            out[c] = ex[c, d1, own_rows]
            out[3 + c] = px[c, d1, own_rows]
            out[15 + c] = hx[c, d1, own_rows]
        for k, i in ((6, d1), (9, d2)):
            out[k] = cx[0, i, own_rows].astype(F32)
            out[k + 1] = cx[1, i, own_rows].astype(F32)
            out[k + 2] = fx[0, i, own_rows]
        for t in range(NY // 8):
            r = slice(R0 + 8 * t, R0 + 8 * t + 8)
            m = cx[0, d2, r]
            kp, bp = pick(tab, m, 2), pick(tab, m, 3)
            for c in range(3):
                out[12 + c, 8 * t:8 * t + 8] = kp * px[c, d2, r] + bp * ex[c, d2, r]

    @pl.when(gx_odd == 0)
    def _():
        slab(out_a, LOW + NX - 1, LOW + NX - 2)
        slab(out_b, LOW, LOW + 1)

    @pl.when(gx_odd == 1)
    def _():
        slab(out_b, LOW + NX - 1, LOW + NX - 2)
        slab(out_a, LOW, LOW + 1)


def near_coefs(e, h, p, mat, via, fill, tab, *refs):
    ex, hx, px, cx, fx, w, sems = refs[5:]
    arrays, ext = (e, h, p, mat, via, fill), (ex, hx, px, cx, fx)
    copies = copy_all(load_pairs(*LATE, arrays, ext, 2, 2), sems.at[pl.ds(0, 6)])
    copies += copy_all(load_pairs(*LATE, arrays, ext, NX - 4, 2), sems.at[pl.ds(6, 6)])
    b = Block(None, None, None, cx, fx, w)
    b.coef(1, tab, OWN)
    b.coef(NX - 2, tab, OWN)
    for copy in copies:
        copy.wait()
    b.coef(2, tab, OWN)
    b.coef(NX - 3, tab, OWN)


def first_edges(row_c, row_d, tab, *refs):
    ex, hx, px, cx, fx, w, out_a, out_b = refs[6:]
    b = Block(ex, hx, px, cx, fx, w)
    b.masks()
    named = {"e": ex, "h": hx, "p": px, "c": cx, "f": fx}
    low = tile_iota(0) < 4
    gy_odd, gx_odd = lax.axis_index("gy") % 2, lax.axis_index("gx") % 2

    def rows_body(x, above_ref, below_ref):
        for k in range(6):
            above, below = above_ref[k, x], below_ref[k, x]
            both = (jnp.where(low, above, pltpu.roll(below, 4, 0)), jnp.where(low, pltpu.roll(above, 4, 0), below))
            for (n, c), tile in zip(ORDER[2 * k:2 * k + 2], both):
                named[n][c, x + LOW, RH:RE] = tile.astype(jnp.int32) if n == "c" else tile
        for c in (0, 2):
            ex[c, x + LOW, RE:RE + 1] = ex[c, x + LOW, R0:R0 + 1]
            hx[c, x + LOW, R0 - 1:R0] = hx[c, x + LOW, RE - 1:RE]

    def all_rows(above_ref, below_ref):
        def body(x, _):
            rows_body(x, above_ref, below_ref)
            return 0

        lax.fori_loop(0, NX, body, 0, unroll=2)

    @pl.when(gy_odd == 0)
    def _():
        all_rows(row_c, row_d)

    @pl.when(gy_odd == 1)
    def _():
        all_rows(row_d, row_c)

    for x in (1, 2, NX - 3, NX - 2):
        b.coef(x, tab, HALO)
    b.h_plane(0)
    for x in (1, 2):
        b.h_plane(x)
        b.e_plane(x)
    b.h_plane(1)
    b.h_plane(NX - 4)
    for x in (NX - 3, NX - 2):
        b.h_plane(x)
        b.e_plane(x)
    b.h_plane(NX - 3)

    n = RE - R0

    def message(out, upward):
        d1, d2, d3 = (LOW + NX - 1, LOW + NX - 2, LOW + NX - 3) if upward else (LOW, LOW + 1, None)
        if upward:
            planes = [(hx, c, d2) for c in range(3)] + [(ex, c, d2) for c in range(3)] + [(hx, c, d3) for c in (1, 2)]
        else:
            planes = [(hx, c, d1) for c in range(3)] + [(hx, c, d2) for c in range(3)] + [(ex, c, d2) for c in (1, 2)]
        for k, (ref, c, i) in enumerate(planes):
            out[n * k:n * k + n] = ref[c, i, R0:RE]
        tiles = [(ex, c, d1) for c in range(3)] + [(px, c, d1) for c in range(3)]
        for i in (d1, d2):
            tiles += [(cx, 0, i), (cx, 1, i), (fx, 0, i)]
        tiles += [(px, c, d2) for c in range(3)] + [(hx, c, d1) for c in range(3)]
        for k, (ref, c, i) in enumerate(tiles):
            at = MSG2 * n + 8 * k
            out[at:at + 8] = ref[c, i, RH:RE].astype(F32)

    @pl.when(gx_odd == 0)
    def _():
        message(out_a, True)
        message(out_b, False)

    @pl.when(gx_odd == 1)
    def _():
        message(out_b, True)
        message(out_a, False)


def interior(e, h, p, mat, via, fill, tab, *refs):
    ex, hx, px, cx, fx, w, sems = refs[6:]
    copies = copy_all(load_pairs(*LATE, (e, h, p, mat, via, fill), (ex, hx, px, cx, fx), 4, NX - 8), sems)
    b = Block(ex, hx, px, cx, fx, w)
    b.masks()
    for x in (0, 3, NX - 4, NX - 1):
        b.coef(x, tab, range(TILES))
    for x in range(4, NX - 4):
        b.coef(x, tab, HALO)
    for copy in copies:
        copy.wait()
    for x in range(4, NX - 4):
        b.coef(x, tab, OWN)
    b.sweep((3, NX - 5), (3, NX - 4))
    b.sweep((2, NX - 4), (2, NX - 3))
    b.sweep((2, NX - 4), (3, NX - 4))
    b.sweep((3, NX - 5), (4, NX - 5), OWN)


def neighbour_cells(got1_a, got1_b, tab, *refs):
    ex, hx, px, cx, fx, w = refs[6:]
    b = Block(ex, hx, px, cx, fx, w)

    def take(m1, below):
        b.take_tiles(below, lambda k: m1[k], slice(R0, RH))

    for_sides(take, (got1_a,), (got1_b,))
    for x in (-2, -1, NX, NX + 1):
        b.coef(x, tab, OWN)


def edge(which, got2, tab, b):
    b.masks()
    n = RE - R0
    above = lax.axis_index("gx") % 2 == which

    def take(below):
        at = MSG2 * n
        b.take_tiles(below, lambda k: got2[at + 8 * k:at + 8 * k + 8], slice(RH, RE))
        d1, d2, d3 = (LOW - 1, LOW - 2, LOW - 3) if below else (LOW + NX, LOW + NX + 1, None)
        if below:
            planes = [(b.h, c, d2) for c in range(3)] + [(b.e, c, d2) for c in range(3)] + [(b.h, c, d3) for c in (1, 2)]
        else:
            planes = [(b.h, c, d1) for c in range(3)] + [(b.h, c, d2) for c in range(3)] + [(b.e, c, d2) for c in (1, 2)]
        for k, (ref, c, i) in enumerate(planes):
            ref[c, i, R0:RE] = got2[n * k:n * k + n]
        for i in (d1, d2):
            for c in (0, 2):
                b.e[c, i, RE:RE + 1] = b.e[c, i, R0:R0 + 1]
                b.h[c, i, R0 - 1:R0] = b.h[c, i, RE - 1:RE]

    @pl.when(above)
    def _():
        take(False)
        for x in (NX, NX + 1):
            b.coef(x, tab, HALO)
        b.sweep((NX - 1, NX - 1), (NX - 1, NX))
        b.sweep((NX - 2, NX), (NX - 2, NX + 1))
        b.sweep((NX - 3, NX), (NX - 3, NX))
        b.sweep((NX - 4, NX - 1), (NX - 4, NX - 1), OWN)

    @pl.when(jnp.logical_not(above))
    def _():
        take(True)
        for x in (-2, -1):
            b.coef(x, tab, HALO)
        b.sweep((-1, -1), (-1, 0))
        b.sweep((-2, 0), (-2, 1))
        b.sweep((-2, 1), (-1, 2))
        b.sweep((-1, 2), (0, 3), OWN)


def edge_a(got2, tab, *refs):
    edge(0, got2, tab, Block(*refs[6:]))


def edge_b(got2, tab, *refs):
    e_out, h_out, p_out, ex, hx, px, cx, fx, w, sems = refs[6:]
    rows = pl.ds(R0, NY)
    done = []

    def store(first, count):
        pairs = []
        for src, dst in ((ex, e_out), (hx, h_out), (px, p_out)):
            pairs.append((src.at[:, pl.ds(LOW + first, count), rows], dst.at[:, pl.ds(first, count)]))
        done.extend(copy_all(pairs, sems.at[pl.ds(len(done), 3)]))

    above = lax.axis_index("gx") % 2 == 1
    store(jnp.where(above, 0, 4), NX - 4)
    edge(1, got2, tab, Block(ex, hx, px, cx, fx, w))
    store(jnp.where(above, NX - 4, 0), 4)
    for copy in done:
        copy.wait()


def shards(efield, hfield, polar, material_map, via_index, fill_fraction, permittivity, conductivity, debye_strength, relax_time, conformal):
    vmem = pl.BlockSpec(memory_space=pltpu.VMEM)
    hbm = pl.BlockSpec(memory_space=pltpu.HBM)
    conformal = conformal.T
    cells = (efield, hfield, polar, material_map, via_index, fill_fraction)
    cells = tuple(pltpu.with_memory_space_constraint(a, pltpu.HBM) for a in cells)
    tables = (permittivity, conductivity, debye_strength, relax_time, conformal)
    tables = tuple(pltpu.with_memory_space_constraint(a, pltpu.HBM) for a in tables)
    shape = jax.ShapeDtypeStruct
    field, slab1 = shape((3,) + EXT, F32), shape((MSG1, NY, NZ), F32)
    slab2, strip = shape((MSG2_ROWS, NZ), F32), shape((6, NX, 8, NZ), F32)
    ints, fill, coef = shape((2,) + EXT, jnp.int32), shape((1,) + EXT, F32), shape((7,) + EXT, F32)
    result = shape((3, NX, NY, NZ), F32)
    params = pltpu.CompilerParams(vmem_limit_bytes=4 << 20)

    ex, hx, px, cx, fx, tab, strip_c, strip_d, slab_a, slab_b = pl.pallas_call(
        load_and_pack, out_shape=(field, field, field, ints, fill, shape((18, 8, NZ), F32), strip, strip, slab1, slab1),
        in_specs=[hbm] * 11, out_specs=(vmem,) * 10,
        scratch_shapes=[pltpu.SMEM((3,), F32)] * 4 + [pltpu.SMEM((3, 8), F32), pltpu.SemaphoreType.DMA((29,))],
        compiler_params=params, name="load_and_pack",
    )(*cells, *tables)
    row_c = swapped(strip_c, "gy", 0)
    row_d = swapped(strip_d, "gy", 1)
    got1_a = swapped(slab_a, "gx", 0)
    got1_b = swapped(slab_b, "gx", 1)
    ex, hx, px, cx, fx, w = pl.pallas_call(
        near_coefs, out_shape=(field, field, field, ints, fill, coef), in_specs=[hbm] * 6 + [vmem] * 6, out_specs=(vmem,) * 6,
        input_output_aliases={7 + k: k for k in range(5)}, scratch_shapes=[pltpu.SemaphoreType.DMA((12,))],
        compiler_params=params, name="near_coefs",
        cost_estimate=pl.CostEstimate(flops=10_000_000, bytes_accessed=4_000_000, transcendentals=0),
    )(*cells, tab, ex, hx, px, cx, fx)
    ex, hx, px, cx, fx, w, send_a, send_b = pl.pallas_call(
        first_edges, out_shape=(field, field, field, ints, fill, coef, slab2, slab2),
        in_specs=[vmem] * 9, out_specs=(vmem,) * 8,
        input_output_aliases={3 + k: k for k in range(6)}, compiler_params=params, name="first_edges",
    )(row_c, row_d, tab, ex, hx, px, cx, fx, w)
    got2_a = swapped(send_a, "gx", 0)
    got2_b = swapped(send_b, "gx", 1)
    state = (ex, hx, px, cx, fx, w)
    shapes = (field, field, field, ints, fill, coef)
    state = pl.pallas_call(
        interior, out_shape=shapes, in_specs=[hbm] * 6 + [vmem] * 7, out_specs=(vmem,) * 6,
        input_output_aliases={7 + k: k for k in range(6)}, scratch_shapes=[pltpu.SemaphoreType.DMA((6,))],
        compiler_params=params, name="interior",
        cost_estimate=pl.CostEstimate(flops=80_000_000, bytes_accessed=20_000_000, transcendentals=0),
    )(*cells, tab, *state)
    state = pl.pallas_call(
        neighbour_cells, out_shape=shapes, in_specs=[vmem] * 9, out_specs=(vmem,) * 6,
        input_output_aliases={3 + k: k for k in range(6)}, compiler_params=params, name="neighbour_cells",
    )(got1_a, got1_b, tab, *state)
    state = pl.pallas_call(
        edge_a, out_shape=shapes, in_specs=[vmem] * 8, out_specs=(vmem,) * 6,
        input_output_aliases={2 + k: k for k in range(6)}, compiler_params=params, name="edge_a",
    )(got2_a, tab, *state)
    outs = pl.pallas_call(
        edge_b, out_shape=(result,) * 3 + shapes, in_specs=[vmem] * 8, out_specs=(hbm,) * 3 + (vmem,) * 6,
        input_output_aliases={2 + k: 3 + k for k in range(6)},
        scratch_shapes=[pltpu.SemaphoreType.DMA((6,))], compiler_params=params, name="edge_b",
    )(got2_b, tab, *state)
    return outs[:3]


def solution(mesh):
    whole, cell = P(None, "gx", "gy", None), P("gx", "gy", None)

    return jax.shard_map(
        shards, mesh=mesh, in_specs=(whole,) * 3 + (cell,) * 3 + (P(),) * 5, out_specs=(whole,) * 3, check_vma=False,
    )
```

```python
import jax
import jax.numpy as jnp
from jax import lax
from jax.experimental import pallas as pl
from jax.experimental.pallas import tpu as pltpu
from jax.sharding import PartitionSpec as P

DT = 0.55
F32 = jnp.float32

NX, NY, NZ = 16, 32, 128
LOW, HIGH = 3, 2
R0, RH, RE = 8, 8 + NY, 16 + NY
EXT = (NX + LOW + HIGH, RE + 8, NZ)
TILES = (RE - R0) // 8
OWN, HALO = range(TILES - 1), range(TILES - 1, TILES)
MSG1, MSG2 = 15, 7
MSG2_ROWS = MSG2 * (RE - R0) + MSG1 * 8

ORDER = (("e", 0), ("e", 1), ("e", 2), ("h", 0), ("h", 1), ("h", 2), ("p", 0), ("p", 1), ("p", 2), ("f", 0), ("c", 0), ("c", 1))


def swapped(value, axis, first):
    pairs = []
    for low in range(first, lax.axis_size(axis) - 1, 2):
        pairs += [(low, low + 1), (low + 1, low)]
    return lax.ppermute(value, axis, pairs)


def tile_iota(dim):
    return lax.broadcasted_iota(jnp.int32, (8, NZ), dim)


def make_tables(perm, cond, stre, rlx, conf, tab):
    for m in range(3):
        tau = jnp.full((8, NZ), rlx[m], F32)
        inv = 1.0 / (2.0 * tau + DT)
        tab[5 * m] = jnp.full((8, NZ), perm[m], F32)
        tab[5 * m + 1] = jnp.full((8, NZ), cond[m] * (DT / 2), F32)
        tab[5 * m + 2] = (2.0 * tau - DT) * inv
        tab[5 * m + 3] = jnp.full((8, NZ), stre[m], F32) * (2.0 * DT) * inv
        tab[5 * m + 4] = 2.0 * DT * inv
    lane = tile_iota(1)
    for c in range(3):
        table = jnp.zeros((8, NZ), F32)
        for v in range(8):
            table = jnp.where(lane == v, conf[c, v], table)
        tab[15 + c] = table


def pick(tab, m, i):
    return jnp.where(m == 0, tab[i], jnp.where(m == 1, tab[5 + i], tab[10 + i]))


class Block:
    def __init__(self, ex, hx, px, cx, fx, w=None):
        self.e, self.h, self.p, self.c, self.f, self.w = ex, hx, px, cx, fx, w

    def masks(self):
        gy = lax.axis_index("gy")
        row = tile_iota(0)
        out = ((row < 4) & (gy == lax.axis_size("gy") - 1)) | ((row >= 4) & (gy == 0))
        self.row_in = jnp.where(out, 0.0, 1.0).astype(F32)
        lane = tile_iota(1)
        self.last, self.first = lane == NZ - 1, lane == 0

    def plane_in(self, x):
        if not isinstance(x, int) or 0 <= x < NX:
            return None
        gx = lax.axis_index("gx")
        out = gx == 0 if x < 0 else gx == lax.axis_size("gx") - 1
        return jnp.where(out, 0.0, 1.0).astype(F32)

    def zf(self, a):
        return jnp.where(self.last, 0.0, pltpu.roll(a, NZ - 1, 1))

    def zb(self, a):
        return jnp.where(self.first, 0.0, pltpu.roll(a, 1, 1))

    def coef(self, x, tab, tiles):
        i = x + LOW
        inside = self.plane_in(x)
        for t in tiles:
            r = slice(R0 + 8 * t, R0 + 8 * t + 8)
            m, v, f = self.c[0, i, r], self.c[1, i, r], self.f[0, i, r]
            pe, s, kp, bp, omk = (pick(tab, m, k) for k in range(5))
            eps = pe * (1.0 + f)
            inv = 1.0 / (eps + s)
            self.w[0, i, r] = (eps - s) * inv - inv * bp
            self.w[1, i, r] = inv * omk
            self.w[2, i, r] = kp
            self.w[3, i, r] = bp
            scale = inv * DT if inside is None else inv * (DT * inside)
            if t == TILES - 1:
                scale = scale * self.row_in
            for c in range(3):
                self.w[4 + c, i, r] = scale * jnp.take_along_axis(tab[15 + c], v, axis=1)

    def take_tiles(self, below, part, rows):
        d1, d2 = (LOW - 1, LOW - 2) if below else (LOW + NX, LOW + NX + 1)
        for c in range(3):
            self.e[c, d1, rows] = part(c)
            self.p[c, d1, rows] = part(3 + c)
            self.w[4 + c, d2, rows] = part(9 + c)
            if below:
                self.h[c, d1, rows] = part(12 + c)
        self.c[0, d1, rows] = part(6).astype(jnp.int32)
        self.c[1, d1, rows] = part(7).astype(jnp.int32)
        self.f[0, d1, rows] = part(8)

    def h_plane(self, x):
        i = x + LOW
        e, h = self.e, self.h
        inside = self.plane_in(x)
        for t in range(TILES):
            a = R0 + 8 * t
            r, up = slice(a, a + 8), slice(a + 1, a + 9)
            e0, e1, e2 = e[0, i, r], e[1, i, r], e[2, i, r]
            m = DT if inside is None else DT * inside
            if t == TILES - 1:
                m = self.row_in * m
            h0 = h[0, i, r] - m * ((e[2, i, up] - e2) - (self.zf(e1) - e1))
            h1 = h[1, i, r] - m * ((self.zf(e0) - e0) - (e[2, i + 1, r] - e2))
            h2 = h[2, i, r] - m * ((e[1, i + 1, r] - e1) - (e[0, i, up] - e0))
            h[0, i, r], h[1, i, r], h[2, i, r] = h0, h1, h2
        h[0, i, R0 - 1:R0] = h0[7:8]
        h[2, i, R0 - 1:R0] = h2[7:8]

    def e_plane(self, x, tiles=range(TILES)):
        i = x + LOW
        e, h, p, w = self.e, self.h, self.p, self.w
        for t in tiles:
            a = R0 + 8 * t
            r, down = slice(a, a + 8), slice(a - 1, a + 7)
            h0, h1, h2 = h[0, i, r], h[1, i, r], h[2, i, r]
            curl = (
                (h2 - h[2, i, down]) - (h1 - self.zb(h1)),
                (h0 - self.zb(h0)) - (h2 - h[2, i - 1, r]),
                (h1 - h[1, i - 1, r]) - (h0 - h[0, i, down]),
            )
            w0, w1, w2, w3 = (w[k, i, r] for k in range(4))
            for c in range(3):
                ec, pc = e[c, i, r], p[c, i, r]
                new = w0 * ec + w1 * pc + w[4 + c, i, r] * curl[c]
                e[c, i, r] = new
                p[c, i, r] = w2 * pc + w3 * ec
                if t == 0 and c != 1 and len(tiles) == TILES:
                    e[c, i, RE:RE + 1] = new[0:1]

    def sweep(self, h_planes, e_planes, tiles=range(TILES)):
        for x in range(min(h_planes[0], e_planes[0]), max(h_planes[1], e_planes[1]) + 1):
            if h_planes[0] <= x <= h_planes[1]:
                self.h_plane(x)
            if e_planes[0] <= x <= e_planes[1]:
                self.e_plane(x, tiles)

    def mask(self, x, t):
        inside = self.plane_in(x)
        m = DT if inside is None else DT * inside
        return self.row_in * m if t == TILES - 1 else m

    def below_second(self):
        i = LOW - 2
        e, h, p, w = self.e, self.h, self.p, self.w
        for t in range(TILES):
            r = slice(R0 + 8 * t, R0 + 8 * t + 8)
            m = self.mask(-2, t)
            h[1, i, r] = e[1, i, r] + m * e[2, i + 1, r]
            h2 = e[2, i, r] - m * e[1, i + 1, r]
            h[2, i, r] = h2
        h[2, i, R0 - 1:R0] = h2[7:8]
        for t in range(TILES):
            a = R0 + 8 * t
            r, down = slice(a, a + 8), slice(a - 1, a + 7)
            h1, h2 = h[1, i, r], h[2, i, r]
            e0 = p[0, i, r] + w[4, i, r] * ((h2 - h[2, i, down]) - (h1 - self.zb(h1)))
            e2 = p[2, i, r] + w[6, i, r] * h1
            e[0, i, r], e[1, i, r], e[2, i, r] = e0, p[1, i, r] - w[5, i, r] * h2, e2
            if t == 0:
                e[0, i, RE:RE + 1] = e0[0:1]
                e[2, i, RE:RE + 1] = e2[0:1]

    def above_second(self):
        i = LOW + NX + 1
        for t in range(TILES):
            r = slice(R0 + 8 * t, R0 + 8 * t + 8)
            self.e[1, i, r] = self.p[1, i, r] + self.w[5, i, r] * self.h[2, i - 1, r]
            self.e[2, i, r] = self.p[2, i, r] - self.w[6, i, r] * self.h[1, i - 1, r]

    def for_above(self, out, tmp):
        i, n = LOW + NX - 2, RE - R0
        e, h, p, w = self.e, self.h, self.p, self.w
        for t in range(TILES):
            a, o = R0 + 8 * t, 8 * t
            r, up = slice(a, a + 8), slice(a + 1, a + 9)
            e0, e1, e2 = e[0, i, r], e[1, i, r], e[2, i, r]
            h1, h2 = h[1, i, r], h[2, i, r]
            m = self.mask(NX - 2, t)
            h0 = h[0, i, r] - m * ((e[2, i, up] - e2) - (self.zf(e1) - e1))
            tmp[r] = h0
            out[o:o + 8] = h1
            out[n + o:n + o + 8] = h2
            out[2 * n + o:2 * n + o + 8] = h1 - m * ((self.zf(e0) - e0) + e2)
            out[3 * n + o:3 * n + o + 8] = h2 + m * (e1 + (e[0, i, up] - e0))
        tmp[R0 - 1:R0] = h0[7:8]
        for t in range(TILES):
            a, o = R0 + 8 * t, 8 * t
            r, down = slice(a, a + 8), slice(a - 1, a + 7)
            h0 = tmp[r]
            w0, w1 = w[0, i, r], w[1, i, r]
            part = [w0 * e[c, i, r] + w1 * p[c, i, r] for c in range(3)]
            part[1] += w[5, i, r] * ((h0 - self.zb(h0)) + h[2, i - 1, r])
            part[2] -= w[6, i, r] * (h[1, i - 1, r] + (h0 - tmp[down]))
            for c in range(3):
                at = (4 + c) * n + o
                out[at:at + 8] = part[c]

    def for_below(self, out):
        i, n = LOW + 1, RE - R0
        e, h, p, w = self.e, self.h, self.p, self.w
        for k, (ref, c, at) in enumerate([(h, c, LOW) for c in range(3)] + [(e, 1, i), (e, 2, i)]):
            out[n * k:n * k + n] = ref[c, at, R0:RE]
        for t in range(TILES):
            a, o = R0 + 8 * t, 8 * t
            r, down = slice(a, a + 8), slice(a - 1, a + 7)
            h0, h1, h2 = h[0, i, r], h[1, i, r], h[2, i, r]
            w0, w1 = w[0, i, r], w[1, i, r]
            part1 = w0 * e[1, i, r] + w1 * p[1, i, r] + w[5, i, r] * ((h0 - self.zb(h0)) - h2)
            part2 = w0 * e[2, i, r] + w1 * p[2, i, r] + w[6, i, r] * (h1 - (h0 - h[0, i, down]))
            out[5 * n + o:5 * n + o + 8] = part1
            out[6 * n + o:6 * n + o + 8] = part2


def for_sides(take, from_a, from_b):
    odd = lax.axis_index("gx") % 2

    @pl.when(odd == 0)
    def _():
        take(*from_a, False)
        take(*from_b, True)

    @pl.when(odd == 1)
    def _():
        take(*from_b, False)
        take(*from_a, True)


def copy_all(pairs, sems):
    copies = [pltpu.make_async_copy(a, b, sems.at[k]) for k, (a, b) in enumerate(pairs)]
    for copy in copies:
        copy.start()
    return copies


LATE = (8, NY - 16)


def load_pairs(at, n, arrays, refs, first, count):
    e, h, p, mat, via, fill = arrays
    ex, hx, px, cx, fx = refs
    planes, there = pl.ds(first, count), pl.ds(at, n)
    dst, here = pl.ds(LOW + first, count), pl.ds(R0 + at, n)
    pairs = [(a.at[:, planes, there], b.at[:, dst, here]) for a, b in ((e, ex), (h, hx), (p, px))]
    return pairs + [(a.at[planes, there], b.at[k, dst, here]) for a, b, k in ((mat, cx, 0), (via, cx, 1), (fill, fx, 0))]


def load_and_pack(e, h, p, mat, via, fill, perm, cond, stre, rlx, conf, ex, hx, px, cx, fx, tab, w, out_c, out_d, out_a, out_b, *scratch):
    smalls, sems = scratch[:5], scratch[5]
    copies = []
    refs = (e, h, p, mat, via, fill), (ex, hx, px, cx, fx)
    for at in (0, NY - 8):
        copies += copy_all(load_pairs(at, 8, *refs, 0, NX), sems.at[pl.ds(len(copies), 6)])
    for first in (0, NX - 4):
        copies += copy_all(load_pairs(*LATE, *refs, first, 4), sems.at[pl.ds(len(copies), 6)])
    few = copy_all(zip((perm, cond, stre, rlx, conf), smalls), sems.at[pl.ds(24, 5)])
    for copy in few:
        copy.wait()
    make_tables(*smalls, tab)
    for copy in copies[:12]:
        copy.wait()
    refs = {"e": ex, "h": hx, "p": px, "c": cx, "f": fx}
    low = tile_iota(0) < 4
    gy_odd, gx_odd = lax.axis_index("gy") % 2, lax.axis_index("gx") % 2

    def strip(x, r, out, upward):
        tiles = [refs[n][c, x + LOW, r:r + 8].astype(F32) for n, c in ORDER]
        for k in range(6):
            a, b = tiles[2 * k], tiles[2 * k + 1]
            if upward:
                out[k, x] = jnp.where(low, pltpu.roll(a, 4, 0), b)
            else:
                out[k, x] = jnp.where(low, a, pltpu.roll(b, 4, 0))

    def strips(up, down):
        def body(x, _):
            strip(x, RH - 8, up, True)
            strip(x, R0, down, False)
            return 0

        lax.fori_loop(0, NX, body, 0, unroll=2)

    @pl.when(gy_odd == 0)
    def _():
        strips(out_c, out_d)

    @pl.when(gy_odd == 1)
    def _():
        strips(out_d, out_c)

    for copy in copies[12:]:
        copy.wait()
    own_rows = slice(R0, RH)

    b = Block(ex, hx, px, cx, fx, w)
    for x in (1, NX - 2):
        b.coef(x, tab, OWN)

    def slab(out, d1, d2):
        for c in range(3):
            out[c] = ex[c, d1, own_rows]
            out[3 + c] = px[c, d1, own_rows]
            out[9 + c] = w[4 + c, d2, own_rows]
            out[12 + c] = hx[c, d1, own_rows]
        out[6] = cx[0, d1, own_rows].astype(F32)
        out[7] = cx[1, d1, own_rows].astype(F32)
        out[8] = fx[0, d1, own_rows]

    @pl.when(gx_odd == 0)
    def _():
        slab(out_a, LOW + NX - 1, LOW + NX - 2)
        slab(out_b, LOW, LOW + 1)

    @pl.when(gx_odd == 1)
    def _():
        slab(out_b, LOW + NX - 1, LOW + NX - 2)
        slab(out_a, LOW, LOW + 1)


def first_edges(row_c, row_d, tab, *refs):
    ex, hx, px, cx, fx, w, out_a, out_b, tmp = refs[6:]
    b = Block(ex, hx, px, cx, fx, w)
    b.masks()
    named = {"e": ex, "h": hx, "p": px, "c": cx, "f": fx}
    low = tile_iota(0) < 4
    gy_odd, gx_odd = lax.axis_index("gy") % 2, lax.axis_index("gx") % 2

    def rows_body(x, above_ref, below_ref):
        for k in range(6):
            above, below = above_ref[k, x], below_ref[k, x]
            both = (jnp.where(low, above, pltpu.roll(below, 4, 0)), jnp.where(low, pltpu.roll(above, 4, 0), below))
            for (n, c), tile in zip(ORDER[2 * k:2 * k + 2], both):
                named[n][c, x + LOW, RH:RE] = tile.astype(jnp.int32) if n == "c" else tile
        for c in (0, 2):
            ex[c, x + LOW, RE:RE + 1] = ex[c, x + LOW, R0:R0 + 1]
            hx[c, x + LOW, R0 - 1:R0] = hx[c, x + LOW, RE - 1:RE]

    def all_rows(above_ref, below_ref):
        def body(x, _):
            rows_body(x, above_ref, below_ref)
            return 0

        lax.fori_loop(0, NX, body, 0, unroll=2)

    @pl.when(gy_odd == 0)
    def _():
        all_rows(row_c, row_d)

    @pl.when(gy_odd == 1)
    def _():
        all_rows(row_d, row_c)

    for x in (1, NX - 2):
        b.coef(x, tab, HALO)
    for x in (2, NX - 3):
        b.coef(x, tab, range(TILES))
    b.h_plane(0)
    for x in (1, 2):
        b.h_plane(x)
        b.e_plane(x)
    b.h_plane(1)
    b.h_plane(NX - 4)
    for x in (NX - 3, NX - 2):
        b.h_plane(x)
        b.e_plane(x)
    b.h_plane(NX - 3)

    n = RE - R0

    def message(out, upward):
        d1, d2 = (LOW + NX - 1, LOW + NX - 2) if upward else (LOW, LOW + 1)
        if upward:
            b.for_above(out, tmp)
        else:
            b.for_below(out)
        tiles = [(ex, c, d1) for c in range(3)] + [(px, c, d1) for c in range(3)]
        tiles += [(cx, 0, d1), (cx, 1, d1), (fx, 0, d1)]
        tiles += [(w, 4 + c, d2) for c in range(3)] + [(hx, c, d1) for c in range(3)]
        for k, (ref, c, i) in enumerate(tiles):
            at = MSG2 * n + 8 * k
            out[at:at + 8] = ref[c, i, RH:RE].astype(F32)

    @pl.when(gx_odd == 0)
    def _():
        message(out_a, True)
        message(out_b, False)

    @pl.when(gx_odd == 1)
    def _():
        message(out_b, True)
        message(out_a, False)


def interior(e, h, p, mat, via, fill, tab, *refs):
    ex, hx, px, cx, fx, w, sems = refs[6:]
    copies = copy_all(load_pairs(*LATE, (e, h, p, mat, via, fill), (ex, hx, px, cx, fx), 4, NX - 8), sems)
    b = Block(ex, hx, px, cx, fx, w)
    b.masks()
    for x in (0, 3, NX - 4, NX - 1):
        b.coef(x, tab, range(TILES))
    for x in range(4, NX - 4):
        b.coef(x, tab, HALO)
    for copy in copies:
        copy.wait()
    for x in range(4, NX - 4):
        b.coef(x, tab, OWN)
    b.sweep((3, NX - 5), (3, NX - 4))
    b.sweep((2, NX - 4), (2, NX - 3))
    b.sweep((2, NX - 4), (3, NX - 4))
    b.sweep((3, NX - 5), (4, NX - 5), OWN)


def neighbour_cells(got1_a, got1_b, tab, *refs):
    ex, hx, px, cx, fx, w = refs[6:]
    b = Block(ex, hx, px, cx, fx, w)

    def take(m1, below):
        b.take_tiles(below, lambda k: m1[k], slice(R0, RH))

    for_sides(take, (got1_a,), (got1_b,))
    for x in (-1, NX):
        b.coef(x, tab, OWN)


def edge(which, got2, tab, b):
    b.masks()
    n = RE - R0
    above = lax.axis_index("gx") % 2 == which

    def take(below):
        at = MSG2 * n
        b.take_tiles(below, lambda k: got2[at + 8 * k:at + 8 * k + 8], slice(RH, RE))
        d1, d2 = (LOW - 1, LOW - 2) if below else (LOW + NX, LOW + NX + 1)
        if below:
            planes = [(b.h, 1, d2), (b.h, 2, d2), (b.e, 1, d2), (b.e, 2, d2)] + [(b.p, c, d2) for c in range(3)]
        else:
            planes = [(b.h, c, d1) for c in range(3)] + [(b.e, 1, d2), (b.e, 2, d2), (b.p, 1, d2), (b.p, 2, d2)]
        for k, (ref, c, i) in enumerate(planes):
            ref[c, i, R0:RE] = got2[n * k:n * k + n]
        for c in (0, 2):
            b.e[c, d1, RE:RE + 1] = b.e[c, d1, R0:R0 + 1]
            b.h[c, d1, R0 - 1:R0] = b.h[c, d1, RE - 1:RE]

    @pl.when(above)
    def _():
        take(False)
        b.coef(NX, tab, HALO)
        b.sweep((NX - 1, NX - 1), (NX - 1, NX))
        b.sweep((NX - 2, NX), (NX - 2, NX))
        b.above_second()
        b.sweep((NX - 3, NX), (NX - 3, NX))
        b.sweep((NX - 4, NX - 1), (NX - 4, NX - 1), OWN)

    @pl.when(jnp.logical_not(above))
    def _():
        take(True)
        b.coef(-1, tab, HALO)
        b.sweep((-1, -1), (-1, 0))
        b.below_second()
        b.sweep((-1, 0), (-1, 1))
        b.sweep((-2, 1), (-1, 2))
        b.sweep((-1, 2), (0, 3), OWN)


def edge_a(got2, tab, *refs):
    edge(0, got2, tab, Block(*refs[6:]))


def edge_b(got2, tab, *refs):
    e_out, h_out, p_out, ex, hx, px, cx, fx, w, sems = refs[6:]
    rows = pl.ds(R0, NY)
    done = []

    def store(first, count):
        pairs = []
        for src, dst in ((ex, e_out), (hx, h_out), (px, p_out)):
            pairs.append((src.at[:, pl.ds(LOW + first, count), rows], dst.at[:, pl.ds(first, count)]))
        done.extend(copy_all(pairs, sems.at[pl.ds(len(done), 3)]))

    above = lax.axis_index("gx") % 2 == 1
    store(jnp.where(above, 0, 4), NX - 4)
    edge(1, got2, tab, Block(ex, hx, px, cx, fx, w))
    store(jnp.where(above, NX - 4, 0), 4)
    for copy in done:
        copy.wait()


def shards(efield, hfield, polar, material_map, via_index, fill_fraction, permittivity, conductivity, debye_strength, relax_time, conformal):
    vmem = pl.BlockSpec(memory_space=pltpu.VMEM)
    hbm = pl.BlockSpec(memory_space=pltpu.HBM)
    conformal = conformal.T
    cells = (efield, hfield, polar, material_map, via_index, fill_fraction)
    cells = tuple(pltpu.with_memory_space_constraint(a, pltpu.HBM) for a in cells)
    tables = (permittivity, conductivity, debye_strength, relax_time, conformal)
    tables = tuple(pltpu.with_memory_space_constraint(a, pltpu.HBM) for a in tables)
    shape = jax.ShapeDtypeStruct
    field, slab1 = shape((3,) + EXT, F32), shape((MSG1, NY, NZ), F32)
    slab2, strip = shape((MSG2_ROWS, NZ), F32), shape((6, NX, 8, NZ), F32)
    ints, fill, coef = shape((2,) + EXT, jnp.int32), shape((1,) + EXT, F32), shape((7,) + EXT, F32)
    result = shape((3, NX, NY, NZ), F32)
    params = pltpu.CompilerParams(vmem_limit_bytes=4 << 20)

    ex, hx, px, cx, fx, tab, w, strip_c, strip_d, slab_a, slab_b = pl.pallas_call(
        load_and_pack, out_shape=(field, field, field, ints, fill, shape((18, 8, NZ), F32), coef, strip, strip, slab1, slab1),
        in_specs=[hbm] * 11, out_specs=(vmem,) * 11,
        scratch_shapes=[pltpu.SMEM((3,), F32)] * 4 + [pltpu.SMEM((3, 8), F32), pltpu.SemaphoreType.DMA((29,))],
        compiler_params=params, name="load_and_pack",
    )(*cells, *tables)
    row_c = swapped(strip_c, "gy", 0)
    row_d = swapped(strip_d, "gy", 1)
    got1_a = swapped(slab_a, "gx", 0)
    got1_b = swapped(slab_b, "gx", 1)
    ex, hx, px, cx, fx, w, send_a, send_b = pl.pallas_call(
        first_edges, out_shape=(field, field, field, ints, fill, coef, slab2, slab2),
        in_specs=[vmem] * 9, out_specs=(vmem,) * 8,
        input_output_aliases={3 + k: k for k in range(6)}, scratch_shapes=[pltpu.VMEM(EXT[1:], F32)],
        compiler_params=params, name="first_edges",
    )(row_c, row_d, tab, ex, hx, px, cx, fx, w)
    got2_a = swapped(send_a, "gx", 0)
    got2_b = swapped(send_b, "gx", 1)
    state = (ex, hx, px, cx, fx, w)
    shapes = (field, field, field, ints, fill, coef)
    state = pl.pallas_call(
        interior, out_shape=shapes, in_specs=[hbm] * 6 + [vmem] * 7, out_specs=(vmem,) * 6,
        input_output_aliases={7 + k: k for k in range(6)}, scratch_shapes=[pltpu.SemaphoreType.DMA((6,))],
        compiler_params=params, name="interior",
        cost_estimate=pl.CostEstimate(flops=80_000_000, bytes_accessed=20_000_000, transcendentals=0),
    )(*cells, tab, *state)
    state = pl.pallas_call(
        neighbour_cells, out_shape=shapes, in_specs=[vmem] * 9, out_specs=(vmem,) * 6,
        input_output_aliases={3 + k: k for k in range(6)}, compiler_params=params, name="neighbour_cells",
    )(got1_a, got1_b, tab, *state)
    state = pl.pallas_call(
        edge_a, out_shape=shapes, in_specs=[vmem] * 8, out_specs=(vmem,) * 6,
        input_output_aliases={2 + k: k for k in range(6)}, compiler_params=params, name="edge_a",
    )(got2_a, tab, *state)
    outs = pl.pallas_call(
        edge_b, out_shape=(result,) * 3 + shapes, in_specs=[vmem] * 8, out_specs=(hbm,) * 3 + (vmem,) * 6,
        input_output_aliases={2 + k: 3 + k for k in range(6)},
        scratch_shapes=[pltpu.SemaphoreType.DMA((6,))], compiler_params=params, name="edge_b",
    )(got2_b, tab, *state)
    return outs[:3]


def solution(mesh):
    whole, cell = P(None, "gx", "gy", None), P("gx", "gy", None)

    return jax.shard_map(
        shards, mesh=mesh, in_specs=(whole,) * 3 + (cell,) * 3 + (P(),) * 5, out_specs=(whole,) * 3, check_vma=False,
    )
```
